32 devices in a mesh: req: 8 (over z, y), tp: 4 (over x, core).
Axes of the slice: x: 2, y: 2, z: 4, core: 2. Of those that a mesh axis runs over, the one named last changes fastest.
Arguments:
- residual: bfloat16 [256, 2048], P('req'), may hold values from -6 to 6
- cache_lengths: int32 [256], P('req'), may hold values from 4 to 4096, as said below
- input_gain: float32 [2048], replicated, may hold values from 0.1 to 1.9
- inner_weight: bfloat16 [2048, 2, 1536], P(None, None, 'tp'), may hold values from -0.125 to 0.125
- step_weight: bfloat16 [2048, 24], P(None, 'tp'), may hold values from -0.125 to 0.125
- step_bias: float32 [24], P('tp'), may hold values from -4 to -1
- decay_log: float32 [24], P('tp'), may hold values from 0 to 2.77
- skip_gain: float32 [24], P('tp'), may hold values from 0.5 to 2
- conv_weight: bfloat16 [4, 1536], P(None, 'tp'), may hold values from -3 to 3
- conv_state: bfloat16 [256, 3, 1536], P('req', None, 'tp'), may hold values from -6 to 6
- coupling_weight: bfloat16 [2048, 512], P(None, 'tp'), may hold values from -0.125 to 0.125
- coupling_conv: bfloat16 [4, 512], P(None, 'tp'), may hold values from -3 to 3
- coupling_state: bfloat16 [256, 3, 512], P('req', None, 'tp'), may hold values from -6 to 6
- scan_state: bfloat16 [256, 24, 64, 256], P('req', 'tp'), may hold values from -30 to 30
- mixer_gain: float32 [1536], P('tp'), may hold values from 0.1 to 1.9
- attention_weight: bfloat16 [2048, 1536], P(None, 'tp'), may hold values from -0.125 to 0.125
- sink_cache: bfloat16 [256, 4, 512], P('req'), may hold values from -2000 to 2000
- window_cache: bfloat16 [256, 1024, 512], P('req', 'tp'), may hold values from -9 to 9
- mamba_out: bfloat16 [1536, 2048], P('tp'), may hold values from -0.15625 to 0.15625
- attention_out: bfloat16 [1024, 2048], P('tp'), may hold values from -0.5 to 0.5
- final_gain: float32 [2048], replicated, may hold values from 0.1 to 1.9
- output_head: bfloat16 [2048, 65536], P(None, ('req', 'tp')), may hold values from -0.375 to 0.375
Outputs:
- new_residual: bfloat16 [256, 2048], P('req', 'tp')
- logits: float32 [256, 65536], P(('req', 'tp'))
- new_scan_state: bfloat16 [256, 24, 64, 256], P('req', 'tp')
- new_conv_state: bfloat16 [256, 3, 1536], P('req', None, 'tp')
- new_coupling_state: bfloat16 [256, 3, 512], P('req', None, 'tp')
- new_key_value: bfloat16 [256, 512], P('req')
The draws below stay inside these ranges and needn't reach their ends.
Inputs may be any that keep to these rules, and one draw needn't show every extreme that they name: `cache_lengths`: A request's cache holds positions 0 to its length - 1; the new token stands at the position equal to the length. Some request has length exactly 4096.
All inputs are finite; a program needn't handle non-finite values.
Results may differ from the reference program's by a relative error of at most 0.02.
Values may be sent and summed in bfloat16 or wider, within the bound.
A program may use at most 128 MiB of HBM per device.

```python
import jax
import jax.numpy as jnp
from jax import lax

D = 2048
MH = 24
MP = 64
NS = 256
CONV = 4
QH = 8
KVH = 2
HD = 128
VOCAB = 65536
WIN = 1024
SINK = 4
MAXLEN = 4096
REQS = 256
DSSM = 1536
QKV = 1536


def draw_cache_lengths(key, part):
    first_draw = jax.random.randint(jax.random.fold_in(key, 11), (REQS,), 0, MAXLEN)
    second_draw = jax.random.randint(jax.random.fold_in(key, 12), (REQS,), 0, MAXLEN)
    drawn = jnp.minimum(SINK + first_draw * second_draw // MAXLEN, MAXLEN)
    chosen = jax.random.randint(jax.random.fold_in(key, 13), (), 0, REQS)
    return jnp.where(jnp.arange(REQS) == chosen, MAXLEN, drawn).astype(jnp.int32)


def draw_scan_state(key, part):
    sampled = jax.random.normal(jax.random.fold_in(key, 21), (REQS, MH, MP, NS), jnp.float32)
    head_level = jnp.arange(MH, dtype=jnp.float32) / max(MH - 1, 1)
    rising = 0.05 * jnp.exp(2.302585 * head_level)
    row_level = jnp.exp(jax.random.uniform(jax.random.fold_in(key, 22), (REQS,), jnp.float32, 0.0, 2.3))
    scaled = sampled * (row_level[:, None] * rising[None, :])[:, :, None, None]
    return jnp.clip(scaled, -29.5, 29.5).astype(jnp.bfloat16)


def draw_sink_cache(key, part):
    half_width = KVH * HD
    sampled = 1.5 * jax.random.normal(jax.random.fold_in(key, 31), (REQS, SINK, 2 * half_width), jnp.float32)
    return jnp.clip(sampled, -1990.0, 1990.0).astype(jnp.bfloat16)


def shard_levels(key, dims, split, low, high):
    loudness = 1.0
    for axis_at, shards_of in split:
        draws = jax.random.uniform(jax.random.fold_in(jax.random.fold_in(key, 6), axis_at), (shards_of,), jnp.float32, low / len(split), high / len(split))
        loudness = loudness * jnp.repeat(jnp.exp(draws), dims[axis_at] // shards_of).reshape((-1,) + (1,) * (len(dims) - 1 - axis_at))
    return loudness


def gaussian(stream_key, shape, scale, most, pieces=(), kind=jnp.bfloat16):
    level = shard_levels(stream_key, shape, pieces, -0.22, 0.18) if pieces else 1.0
    values = jax.random.normal(stream_key, shape, jnp.float32) * scale * level
    return jnp.minimum(jnp.maximum(values, -most), most).astype(kind)


def setup_inputs(seed: int = 0) -> dict:
    streams_of = jax.random.split(jax.random.key(seed), 23)
    return {
        "residual": gaussian(streams_of[0], (REQS, D), 1.0, 6.0, ((0, 8),)),
        "cache_lengths": draw_cache_lengths(jax.random.fold_in(streams_of[22], 71), 0),
        "input_gain": jnp.clip(1.0 + 0.18 * jax.random.normal(streams_of[2], (D,), jnp.float32), 0.1, 1.9),
        "inner_weight": gaussian(streams_of[3], (D, 2, DSSM), D ** -0.5, 0.125, ((2, 4),)),
        "step_weight": gaussian(streams_of[4], (D, MH), D ** -0.5, 0.125, ((1, 4),)),
        "step_bias": jnp.clip(-4.0 + 3.0 * jax.random.uniform(streams_of[5], (MH,), jnp.float32) ** shard_levels(streams_of[5], (MH,), ((0, 4),), -0.2, 0.2), -4.0, -1.0),
        "decay_log": jnp.clip(2.77 * jax.random.uniform(streams_of[6], (MH,), jnp.float32) ** shard_levels(streams_of[6], (MH,), ((0, 4),), -0.2, 0.2), 0.0, 2.77),
        "skip_gain": jnp.clip(0.5 + 1.5 * jax.random.uniform(streams_of[7], (MH,), jnp.float32) ** shard_levels(streams_of[7], (MH,), ((0, 4),), -0.2, 0.2), 0.5, 2.0),
        "conv_weight": gaussian(streams_of[8], (CONV, DSSM), CONV ** -0.5, 3.0, ((1, 4),)),
        "conv_state": gaussian(streams_of[9], (REQS, CONV - 1, DSSM), 1.0, 6.0, ((0, 8), (2, 4))),
        "coupling_weight": gaussian(streams_of[10], (D, 2 * NS), D ** -0.5, 0.125, ((1, 4),)),
        "coupling_conv": gaussian(streams_of[11], (CONV, 2 * NS), CONV ** -0.5, 3.0, ((1, 4),)),
        "coupling_state": gaussian(streams_of[12], (REQS, CONV - 1, 2 * NS), 1.0, 6.0, ((0, 8), (2, 4))),
        "scan_state": draw_scan_state(jax.random.fold_in(streams_of[22], 71), 0),
        "mixer_gain": jnp.clip(1.0 + 0.18 * jax.random.normal(streams_of[14], (DSSM,), jnp.float32), 0.1, 1.9),
        "attention_weight": gaussian(streams_of[15], (D, QKV), D ** -0.5, 0.125, ((1, 4),)),
        "sink_cache": draw_sink_cache(jax.random.fold_in(streams_of[22], 71), 0),
        "window_cache": gaussian(streams_of[17], (REQS, WIN, 2 * KVH * HD), 1.5, 9.0, ((0, 8), (1, 4))),
        "mamba_out": gaussian(streams_of[18], (DSSM, D), DSSM ** -0.5, 0.15625, ((0, 4),)),
        "attention_out": gaussian(streams_of[19], (QH * HD, D), HD ** -0.5, 0.5, ((0, 4),)),
        "final_gain": jnp.clip(1.0 + 0.18 * jax.random.normal(streams_of[20], (D,), jnp.float32), 0.1, 1.9),
        "output_head": gaussian(streams_of[21], (D, VOCAB), (D // 9) ** -0.5, 0.375, ((1, 32),)),
    }


EPSILON = 1e-05

def rounded(values):
    return lax.optimization_barrier(values.astype(jnp.bfloat16))

def rms_rows(values, gain):
    widened = values.astype(jnp.float32)
    mean_sq = lax.optimization_barrier(jnp.mean(widened * widened, axis=-1, keepdims=True))
    return (widened * lax.rsqrt(mean_sq + EPSILON) * gain).astype(jnp.bfloat16)

def conv_apply(old_state, fresh_row, taps):
    window = jnp.concatenate([old_state, fresh_row[:, None, :]], axis=1)
    mixed_rows = jnp.einsum('rkc,kc->rc', window.astype(jnp.float32), taps.astype(jnp.float32), precision=lax.Precision.HIGHEST)
    return (jax.nn.silu(mixed_rows), window[:, 1:, :])

def scan_request(operands):
    old_state, x_heads, step_size, decay_rate, input_vec, output_vec = operands
    updated = decay_rate[:, None, None] * old_state.astype(jnp.float32) + (step_size[:, None] * x_heads)[:, :, None] * input_vec[None, None, :]
    readout = jnp.einsum('hpn,n->hp', updated, output_vec, precision=lax.Precision.HIGHEST)
    return (updated.astype(jnp.bfloat16), readout)

def attend_request(operands):
    qkv_row, sinks, window_rows, length = operands
    half_width = KVH * HD
    queries = qkv_row[:QH * HD].reshape(KVH, QH // KVH, HD).astype(jnp.float32)
    fresh_row = qkv_row[QH * HD:].reshape(1, 2 * half_width)
    stacked = jnp.concatenate([sinks, window_rows, fresh_row], axis=0).astype(jnp.float32)
    key_rows = stacked[:, :half_width].reshape(-1, KVH, HD)
    value_rows = stacked[:, half_width:].reshape(-1, KVH, HD)
    slot_index = jnp.arange(WIN, dtype=jnp.int32)
    back_steps = (length - 1 - slot_index) % WIN
    live_slots = (length - 1 - back_steps >= SINK) & (back_steps != WIN - 1)
    valid_mask = jnp.concatenate([jnp.ones((SINK,), dtype=jnp.bool_), live_slots, jnp.ones((1,), dtype=jnp.bool_)])
    scores = jnp.einsum('kgd,skd->kgs', queries, key_rows, precision=lax.Precision.HIGHEST) * HD ** (-0.5)
    masked = jnp.where(valid_mask, scores, -jnp.inf)
    row_peak = lax.optimization_barrier(jnp.max(masked, axis=-1, keepdims=True))
    weights = jnp.where(valid_mask, jnp.exp(masked - row_peak), 0.0)
    totals = lax.optimization_barrier(jnp.sum(weights, axis=-1))
    summed = jnp.einsum('kgs,skd->kgd', rounded(weights).astype(jnp.float32), value_rows, precision=lax.Precision.HIGHEST)
    return (summed / totals[..., None]).reshape(QH * HD).astype(jnp.bfloat16)

def reference(residual, cache_lengths, input_gain, inner_weight, step_weight, step_bias, decay_log, skip_gain, conv_weight, conv_state, coupling_weight, coupling_conv, coupling_state, scan_state, mixer_gain, attention_weight, sink_cache, window_cache, mamba_out, attention_out, final_gain, output_head):
    units = MH * MP
    normed = rms_rows(residual, input_gain)
    projected = rounded(jnp.dot(normed, inner_weight.reshape(D, 2 * units), preferred_element_type=jnp.float32))
    gate_rows = projected[:, :units]
    x_rows, new_conv_state = conv_apply(conv_state, projected[:, units:], conv_weight)
    step_rows = rounded(jnp.dot(normed, step_weight, preferred_element_type=jnp.float32))
    step_size = jax.nn.softplus(step_rows.astype(jnp.float32) + step_bias)
    decay_rate = jnp.exp(-step_size * jnp.exp(decay_log))
    coupling_pre = rounded(jnp.dot(normed, coupling_weight, preferred_element_type=jnp.float32))
    coupling_rows, new_coupling_state = conv_apply(coupling_state, coupling_pre, coupling_conv)
    coupling_rows = rounded(coupling_rows).astype(jnp.float32)
    x_heads = x_rows.reshape(REQS, MH, MP)
    new_scan_state, readout = lax.map(scan_request, (scan_state, x_heads, step_size, decay_rate, coupling_rows[:, :NS], coupling_rows[:, NS:]))
    readout = readout + skip_gain[None, :, None] * x_heads
    gated_rows = readout.reshape(REQS, units) * jax.nn.silu(gate_rows.astype(jnp.float32))
    mean_sq = lax.optimization_barrier(jnp.mean(gated_rows * gated_rows, axis=1, keepdims=True))
    mamba_rows = (gated_rows * lax.rsqrt(mean_sq + EPSILON) * mixer_gain).astype(jnp.bfloat16)
    qkv_rows = rounded(jnp.dot(normed, attention_weight, preferred_element_type=jnp.float32))
    new_key_value = qkv_rows[:, QH * HD:]
    attended = lax.map(attend_request, (qkv_rows, sink_cache, window_cache, cache_lengths))
    mixed_rows = jnp.dot(mamba_rows, mamba_out, preferred_element_type=jnp.float32) + jnp.dot(attended, attention_out, preferred_element_type=jnp.float32)
    new_residual = (residual.astype(jnp.float32) + mixed_rows).astype(jnp.bfloat16)
    final_rows = rms_rows(new_residual, final_gain)
    logits = jnp.dot(final_rows, output_head, preferred_element_type=jnp.float32)
    return (new_residual, logits, new_scan_state, new_conv_state, new_coupling_state, new_key_value)
```

```python
import functools

import jax
import jax.numpy as jnp
from jax import lax
from jax.experimental import pallas as pl
from jax.experimental.pallas import tpu as pltpu
from jax.sharding import PartitionSpec as P

MH = 24
MP = 64
NS = 256
QH = 8
KVH = 2
HD = 128
WIN = 1024
SINK = 4
BR = 8

EPSILON = 1e-05
NEG_BIG = -1e30
MESH = pl.DeviceIdType.MESH
NT = (((1,), (1,)), ((), ()))


def norm_rows(values, gain):
    widened = values.astype(jnp.float32)
    mean_sq = jnp.mean(widened * widened, axis=-1, keepdims=True)
    return (widened * lax.rsqrt(mean_sq + EPSILON) * gain).astype(jnp.bfloat16)


def silu(v):
    return v / (1.0 + jnp.exp(-v))


def conv_rows(old, fresh, taps_ref):
    steps = [row.astype(jnp.float32) for row in (*old, fresh)]
    taps = taps_ref[...].astype(jnp.float32)
    mixed = steps[0] * taps[0:1]
    for k in range(1, 4):
        mixed = mixed + steps[k] * taps[k : k + 1]
    return silu(mixed)


def by_head(ref, g, shape):
    lane = lax.broadcasted_iota(jnp.int32, shape, 1)
    return jnp.where(lane < MP, ref[2 * g], ref[2 * g + 1])


def entry_kernel(
    tp_size, bias_ref, log_ref, residual_ref, gain_ref, attention_ref, coupling_ref, taps_ref,
    state_ref, step_weight_ref, normed_ref, pre_ref, qkv_ref, coup_ref, step_ref, decay_ref,
    qkv_s, qkv_r, coup_s, coup_r,
):
    r = lax.axis_index("req")
    t = lax.axis_index("tp")
    peers = [lax.rem(t + k, tp_size) for k in range(tp_size)]
    barrier = pltpu.get_barrier_semaphore()
    for k in range(1, tp_size):
        pl.semaphore_signal(barrier, inc=1, device_id=(r, peers[k]), device_id_type=MESH)
    normed = norm_rows(residual_ref[...], gain_ref[...])
    normed_ref[...] = normed
    copies = []

    def share(out_ref, value, ssem, rsem):
        width = value.shape[1]
        cols = pl.ds(pl.multiple_of(t * width, 128), width)
        out_ref[:, cols] = value
        for k in range(1, tp_size):
            copy = pltpu.make_async_remote_copy(
                src_ref=out_ref.at[:, cols], dst_ref=out_ref.at[:, cols], send_sem=ssem.at[k],
                recv_sem=rsem.at[k], device_id=(r, peers[k]), device_id_type=MESH,
            )
            copy.start()
            copies.append(copy)

    qkv = jnp.dot(normed, attention_ref[...], preferred_element_type=jnp.float32)
    pl.semaphore_wait(barrier, tp_size - 1)
    share(qkv_ref, qkv.astype(jnp.bfloat16), qkv_s, qkv_r)
    pre = jnp.dot(normed, coupling_ref[...], preferred_element_type=jnp.float32).astype(jnp.bfloat16)
    pre_ref[...] = pre
    share(coup_ref, conv_rows([state_ref[k] for k in range(3)], pre, taps_ref).astype(jnp.bfloat16), coup_s, coup_r)
    steps = (
        lax.dot_general(normed, step_weight_ref[...], NT, preferred_element_type=jnp.float32)
        .astype(jnp.bfloat16)
        .astype(jnp.float32)
    )
    shape = (normed.shape[0], 2 * MP)
    for g in range(steps.shape[1] // 2):
        lane = lax.broadcasted_iota(jnp.int32, shape, 1)
        v = jnp.where(lane < MP, steps[:, 2 * g : 2 * g + 1], steps[:, 2 * g + 1 : 2 * g + 2])
        v = v + by_head(bias_ref, g, shape)
        size = jnp.maximum(v, 0.0) + jnp.log1p(jnp.exp(-jnp.abs(v)))
        step_ref[:, g * 2 * MP : (g + 1) * 2 * MP] = size
        decay_ref[:, g * 2 * MP : (g + 1) * 2 * MP] = jnp.exp(
            -size * jnp.exp(by_head(log_ref, g, shape))
        )
    for copy in copies:
        copy.wait()


def entry(bias, decay_log, residual, gain, attention_weight, coupling_weight, taps, state, step_weight):
    tp_size = lax.axis_size("tp")
    rows, model = residual.shape
    units = bias.shape[0] * MP
    vmem = pl.BlockSpec(memory_space=pltpu.VMEM)
    smem = pl.BlockSpec(memory_space=pltpu.SMEM)
    dma = pltpu.SemaphoreType.DMA((tp_size,))
    shaped = jax.ShapeDtypeStruct
    return pl.pallas_call(
        functools.partial(entry_kernel, tp_size),
        in_specs=[smem] * 2 + [vmem] * 7,
        out_specs=[vmem] * 6,
        out_shape=[
            shaped((rows, model), jnp.bfloat16),
            shaped((rows, coupling_weight.shape[1]), jnp.bfloat16),
            shaped((rows, attention_weight.shape[1] * tp_size), jnp.bfloat16),
            shaped((rows, coupling_weight.shape[1] * tp_size), jnp.bfloat16),
            shaped((rows, units), jnp.float32),
            shaped((rows, units), jnp.float32),
        ],
        scratch_shapes=[dma] * 4,
        compiler_params=pltpu.CompilerParams(
            collective_id=0, has_side_effects=True, vmem_limit_bytes=60 << 20
        ),
    )(bias, decay_log, residual, gain[None], attention_weight, coupling_weight, taps, state, step_weight)


def mixer_kernel(
    len_ref, skip_ref, qkv_ref, sink_ref, window_ref, state_ref, coup_ref, pre_ref, coup_state_ref,
    projected_ref, taps_ref, conv_state_ref, step_ref, decay_ref, new_state_ref, new_conv_ref,
    new_coup_ref, key_value_ref, summed_ref, stats_ref, gated_ref, heads_scr, stat_scr, extra_scr,
):
    half = KVH * HD
    group = QH // KVH
    i = pl.program_id(0)
    t = lax.axis_index("tp")
    units = step_ref.shape[2]
    slots = window_ref.shape[1]
    coup = coup_ref[i]
    out_rows = coup[:, NS:]
    in_f32 = coup[:, :NS].astype(jnp.float32)
    qkv = qkv_ref[i]
    fresh = qkv[:, QH * HD :]
    key_value_ref[i] = fresh

    for h in range(QH):
        heads_scr[pl.ds(h, BR, stride=QH), :] = qkv[:, h * HD : (h + 1) * HD].astype(jnp.float32)
    for j in range(BR):
        extra_scr[j * SINK : (j + 1) * SINK, :] = sink_ref[i * BR + j].astype(jnp.float32)
    extra_scr[BR * SINK : BR * SINK + BR, :] = fresh.astype(jnp.float32)
    extra_scr[BR * SINK + BR :, :] = jnp.zeros_like(extra_scr[BR * SINK + BR :, :])
    extra = extra_scr[...].astype(jnp.bfloat16)
    head_row = lax.broadcasted_iota(jnp.int32, (BR * QH, HD), 0) % QH
    lane = lax.broadcasted_iota(jnp.int32, (BR * QH, HD), 1)
    first_half = head_row < group
    q = heads_scr[...]
    wide = jnp.concatenate([jnp.where(first_half, q, 0.0), jnp.where(first_half, 0.0, q)], axis=1)
    block = lambda array, j: array[j * QH : (j + 1) * QH]
    slot = t * slots + lax.broadcasted_iota(jnp.int32, (QH, slots), 1)
    lives, scores = [], []
    for j in range(BR):
        last = len_ref[i * BR + j] - 1
        back = jnp.bitwise_and(last - slot, WIN - 1)
        lives.append((last - back >= SINK) & (back != WIN - 1))
        raw = lax.dot_general(
            block(wide, j).astype(jnp.bfloat16), window_ref[j, :, :half], NT,
            preferred_element_type=jnp.float32,
        )
        scores.append(jnp.where(lives[j], raw * HD ** (-0.5), NEG_BIG))
    s1 = jnp.concatenate(scores, axis=0)
    s2 = lax.dot_general(
        wide.astype(jnp.bfloat16), extra[:, :half], NT, preferred_element_type=jnp.float32
    ) * HD ** (-0.5)
    col = lax.broadcasted_iota(jnp.int32, s2.shape, 1)
    owner = lax.broadcasted_iota(jnp.int32, s2.shape, 0) // QH
    live2 = (jnp.where(col < BR * SINK, col // SINK, col - BR * SINK) == owner) & (t == 0)
    s2 = jnp.where(live2, s2, NEG_BIG)
    peak = jnp.maximum(jnp.max(s1, axis=1, keepdims=True), jnp.max(s2, axis=1, keepdims=True))
    w1 = jnp.exp(s1 - peak)
    w1 = jnp.concatenate([jnp.where(lives[j], block(w1, j), 0.0) for j in range(BR)], axis=0)
    w2 = jnp.where(live2, jnp.exp(s2 - peak), 0.0)
    total = jnp.sum(w1, axis=1, keepdims=True) + jnp.sum(w2, axis=1, keepdims=True)
    acc = jnp.concatenate(
        [
            jnp.dot(
                block(w1, j).astype(jnp.bfloat16), window_ref[j, :, half:],
                preferred_element_type=jnp.float32,
            )
            for j in range(BR)
        ],
        axis=0,
    ) + jnp.dot(w2.astype(jnp.bfloat16), extra[:, half:], preferred_element_type=jnp.float32)
    heads_scr[...] = jnp.where(first_half, acc[:, :HD], acc[:, HD:])
    stat_scr[...] = jnp.where(lane == head_row, peak, 0.0) + jnp.where(
        lane == head_row + QH, total, 0.0
    )
    stats = functools.reduce(jnp.add, [stat_scr[pl.ds(h, BR, stride=QH), :] for h in range(QH)])
    per_chunk = summed_ref.shape[3] // HD
    for h in range(QH):
        summed_ref[h // per_chunk, i, :, (h % per_chunk) * HD : (h % per_chunk + 1) * HD] = heads_scr[
            pl.ds(h, BR, stride=QH), :
        ].astype(jnp.bfloat16)

    gate = projected_ref[0, i].astype(jnp.float32)
    x_pre = projected_ref[1, i]
    x = conv_rows([conv_state_ref[k, i] for k in range(3)], x_pre, taps_ref)
    new_conv_ref[0, i] = conv_state_ref[1, i]
    new_conv_ref[1, i] = conv_state_ref[2, i]
    new_conv_ref[2, i] = x_pre
    new_coup_ref[0, i] = coup_state_ref[1, i]
    new_coup_ref[1, i] = coup_state_ref[2, i]
    new_coup_ref[2, i] = pre_ref[i]
    step_x = step_ref[i] * x
    decay = decay_ref[i]
    both = jnp.sum(in_f32 * out_rows.astype(jnp.float32), axis=1, keepdims=True)
    step_x_t = step_x.T
    decay_t = decay.T
    read_rows = []
    for j in range(BR):
        state = state_ref[j]
        read_rows.append(
            lax.dot_general(out_rows, state, NT, preferred_element_type=jnp.float32)[j : j + 1, :]
        )
        new_state_ref[j] = (
            decay_t[:, j : j + 1] * state.astype(jnp.float32)
            + step_x_t[:, j : j + 1] * in_f32[j : j + 1, :]
        ).astype(jnp.bfloat16)
    readout = decay * jnp.concatenate(read_rows, axis=0) + step_x * both
    skip = jnp.concatenate(
        [by_head(skip_ref, g, (BR, 2 * MP)) for g in range(units // (2 * MP))], axis=1
    )
    gated = (readout + skip * x) * silu(gate)
    gated_ref[i] = gated
    square = jnp.sum(gated * gated, axis=1, keepdims=True)
    stats_ref[i] = jnp.where(
        lax.broadcasted_iota(jnp.int32, stats.shape, 1) == 2 * QH, square, stats
    )


def mixer(
    lengths, skip, qkv, sink, window, state, coup, pre, coup_state, projected, taps, conv_state,
    step, decay, tp_size,
):
    rows, units = step.shape
    blocks = rows // BR

    def split(a):
        at = a.ndim - 2
        return a.reshape(a.shape[:at] + (blocks, BR) + a.shape[at + 1 :])

    whole = lambda shape: pl.BlockSpec(shape, lambda i: (0,) * len(shape))
    cube = lambda a: pl.BlockSpec((BR,) + a.shape[1:], lambda i: (i, 0, 0))
    smem = pl.BlockSpec(memory_space=pltpu.SMEM)
    chunk = QH * HD // tp_size
    small = [split(a) for a in (coup, pre, coup_state, projected)]
    late = [split(a) for a in (conv_state, step, decay)]
    qkv = split(qkv)
    outs = [
        ((3, blocks, BR, units), jnp.bfloat16),
        ((3, blocks, BR, coup_state.shape[2]), jnp.bfloat16),
        ((blocks, BR, 2 * KVH * HD), jnp.bfloat16),
        ((tp_size, blocks, BR, chunk), jnp.bfloat16),
        ((blocks, BR, 128), jnp.float32),
        ((blocks, BR, units), jnp.float32),
    ]
    results = pl.pallas_call(
        mixer_kernel,
        grid=(blocks,),
        in_specs=[smem, smem, whole(qkv.shape), whole(sink.shape), cube(window), cube(state)]
        + [whole(a.shape) for a in small]
        + [whole(taps.shape)]
        + [whole(a.shape) for a in late],
        out_specs=[cube(state)] + [whole(shape) for shape, _ in outs],
        out_shape=[jax.ShapeDtypeStruct(state.shape, jnp.bfloat16)]
        + [jax.ShapeDtypeStruct(shape, kind) for shape, kind in outs],
        scratch_shapes=[
            pltpu.VMEM((BR * QH, HD), jnp.float32),
            pltpu.VMEM((BR * QH, HD), jnp.float32),
            pltpu.VMEM((BR * QH, 2 * KVH * HD), jnp.float32),
        ],
        compiler_params=pltpu.CompilerParams(vmem_limit_bytes=60 << 20),
    )(lengths, skip, qkv, sink, window, state, *small, taps, *late)
    merge = lambda a: a.reshape(a.shape[:-3] + (rows, a.shape[-1]))
    return [results[0]] + [merge(a) for a in results[1:]]


def other(index, k):
    bit = 1
    while bit <= k:
        if k & bit:
            index = index + bit - 2 * bit * lax.rem(lax.div(index, bit), 2)
        bit *= 2
    return index


def joint_kernel(
    tp_size, req_size, summed_ref, stats_ref, gated_ref, mixer_gain_ref, residual_ref, final_gain_ref,
    mamba_out_ref, attention_out_ref, head_ref, new_residual_ref, logits_ref, mamba_buf, attention_buf,
    sum_buf, stat_buf, part_out, part_buf, gather, final_buf, head_buf, logit_out,
    sum_s, sum_r, stat_s, stat_r, part_s, part_r, gat_s, gat_r, log_s, log_r, load_sem,
):
    r = lax.axis_index("req")
    t = lax.axis_index("tp")
    rows = gated_ref.shape[0]
    width = new_residual_ref.shape[1]
    peers = [other(t, q) for q in range(tp_size)]
    reqs = [other(r, k) for k in range(req_size)]
    barrier = pltpu.get_barrier_semaphore()
    for q in range(1, tp_size):
        pl.semaphore_signal(barrier, inc=1, device_id=(r, peers[q]), device_id_type=MESH)
    for k in range(1, req_size):
        pl.semaphore_signal(barrier, inc=1, device_id=(reqs[k], t), device_id_type=MESH)
    loads = [
        pltpu.make_async_copy(src, dst, load_sem.at[n])
        for n, (src, dst) in enumerate(
            [(mamba_out_ref, mamba_buf), (attention_out_ref, attention_buf), (head_ref, head_buf)]
        )
    ]
    for load in loads:
        load.start()
    pl.semaphore_wait(barrier, tp_size + req_size - 2)

    def send(src, dst, ssem, rsem, where):
        copy = pltpu.make_async_remote_copy(
            src_ref=src, dst_ref=dst, send_sem=ssem, recv_sem=rsem,
            device_id=where, device_id_type=MESH,
        )
        copy.start()
        return copy

    first = []
    for q in reversed(range(1, tp_size)):
        where = (r, peers[q])
        first.append(send(stats_ref, stat_buf.at[q], stat_s.at[q], stat_r.at[q], where))
        first.append(send(summed_ref.at[peers[q]], sum_buf.at[q], sum_s.at[q], sum_r.at[q], where))
    mamba = (gated_ref[...] * mixer_gain_ref[...]).astype(jnp.bfloat16)
    columns = lambda p: pl.ds(pl.multiple_of(p * width, 128), width)
    loads[0].wait()
    unscaled = [
        jnp.dot(mamba, mamba_buf[:, columns(peers[q])], preferred_element_type=jnp.float32)
        for q in range(tp_size)
    ]
    loads[1].wait()
    for copy in first:
        copy.wait()
    stats = [stats_ref[...]] + [stat_buf[q] for q in range(1, tp_size)]
    sums = [summed_ref[t].astype(jnp.float32)] + [
        sum_buf[q].astype(jnp.float32) for q in range(1, tp_size)
    ]
    lane = lax.broadcasted_iota(jnp.int32, (rows, 128), 1)
    local_heads = QH // tp_size
    pieces = []
    for hl in range(local_heads):
        h = t * local_heads + hl
        peaks = [jnp.sum(jnp.where(lane == h, s, 0.0), axis=1, keepdims=True) for s in stats]
        totals = [jnp.sum(jnp.where(lane == h + QH, s, 0.0), axis=1, keepdims=True) for s in stats]
        top = functools.reduce(jnp.maximum, peaks)
        scales = [jnp.exp(p - top) for p in peaks]
        below = functools.reduce(jnp.add, [a * b for a, b in zip(scales, totals)])
        above = functools.reduce(
            jnp.add, [a * b[:, hl * HD : (hl + 1) * HD] for a, b in zip(scales, sums)]
        )
        pieces.append((above / below).astype(jnp.bfloat16))
    attended = jnp.concatenate(pieces, axis=1)
    square = functools.reduce(jnp.add, [s[:, 2 * QH : 2 * QH + 1] for s in stats])
    mamba_scale = lax.rsqrt(square / (MH * MP) + EPSILON)

    def partial(q):
        return mamba_scale * unscaled[q] + jnp.dot(
            attended, attention_buf[:, columns(peers[q])], preferred_element_type=jnp.float32
        )

    second = {}
    for q in reversed(range(1, tp_size)):
        part_out[q] = partial(q).astype(jnp.bfloat16)
        second[q] = send(part_out.at[q], part_buf.at[q], part_s.at[q], part_r.at[q], (r, peers[q]))
    mixed = residual_ref[:, columns(t)].astype(jnp.float32) + partial(0)
    for q in range(1, tp_size):
        second[q].wait()
        mixed = mixed + part_buf[q].astype(jnp.float32)
    fresh = mixed.astype(jnp.bfloat16)
    new_residual_ref[...] = fresh
    gather[0, 0] = fresh

    half = req_size // 2
    far_groups = list(range(half, req_size))
    near_groups = list(range(2, half)) + [1]
    along, over, near, far = {}, {}, {}, {}
    for k in far_groups + near_groups:
        along[k] = send(
            gather.at[0, 0], gather.at[k, 0], gat_s.at[k, 0], gat_r.at[k, 0], (reqs[k], t)
        )

    def spread(k):
        if k:
            along[k].wait_recv()
        over[k] = send(
            gather.at[k, 0], gather.at[k, 2], gat_s.at[k, 2], gat_r.at[k, 2], (r, peers[2])
        )
        near[k] = send(
            gather.at[k, 0], gather.at[k, 1], gat_s.at[k, 1], gat_r.at[k, 1], (r, peers[1])
        )

    def pair_up(k):
        over[k].wait_recv()
        far[k] = send(
            gather.at[k, 2], gather.at[k, 3], gat_s.at[k, 3], gat_r.at[k, 3], (r, peers[1])
        )

    vocab = head_buf.shape[1]
    tile = min(512, vocab)
    each = rows // tp_size
    source = r * tp_size + t
    sent = []

    def project(groups):
        for k in groups:
            near[k].wait_recv()
            far[k].wait_recv()
            values = [gather[k, i].astype(jnp.float32) for i in range(tp_size)]
            mean = functools.reduce(
                jnp.add, [jnp.sum(v * v, axis=1, keepdims=True) for v in values]
            ) / (width * tp_size)
            scale = lax.rsqrt(mean + EPSILON)
            for i in range(tp_size):
                cols = columns(peers[i])
                final_buf[k * rows : (k + 1) * rows, cols] = (
                    values[i] * scale * final_gain_ref[:, cols]
                ).astype(jnp.bfloat16)
        low = groups[0] * rows
        high = low + len(groups) * rows

        def head_tile(c, carry):
            cols = pl.ds(pl.multiple_of(c * tile, 128), tile)
            part = jnp.dot(
                final_buf[low:high, :], head_buf[:, cols], preferred_element_type=jnp.float32
            )
            for n, k in enumerate(groups):
                for q in range(tp_size):
                    at = n * rows + q * each
                    logit_out[k, q, :, cols] = part[at : at + each, :].astype(jnp.bfloat16)
            return carry

        lax.fori_loop(0, vocab // tile, head_tile, 0)
        for k in groups:
            for q in reversed(range(tp_size)):
                if k or q:
                    sent.append(
                        send(
                            logit_out.at[k, peers[q]], logits_ref.at[source], log_s.at[k, q],
                            log_r.at[k, q], (reqs[k], peers[q]),
                        )
                    )

    early, rest = far_groups[:2], far_groups[2:]
    spread(0)
    for k in early:
        spread(k)
    pair_up(0)
    loads[2].wait()
    project([0])
    own = pltpu.make_async_copy(logit_out.at[0, t], logits_ref.at[source], load_sem.at[3])
    own.start()
    for k in rest + near_groups:
        spread(k)
    for k in early:
        pair_up(k)
    for n, k in enumerate(early):
        project([k])
        if n == 0:
            for later in rest:
                pair_up(later)
    for k in near_groups:
        pair_up(k)
    for k in rest[::2]:
        project([k, k + 1])
    for k in near_groups[:-1:2]:
        project([k, k + 1])
    project([1])
    own.wait()
    for copy in sent:
        copy.wait()
    for copies in (along, over, near, far):
        for copy in copies.values():
            copy.wait_send()


def joint(
    summed, stats, gated, mixer_gain, mamba_out, attention_out, residual, final_gain, output_head
):
    tp_size = lax.axis_size("tp")
    req_size = lax.axis_size("req")
    rows, model = residual.shape
    width = model // tp_size
    chunk = summed.shape[2]
    each = rows // tp_size
    vocab = output_head.shape[1]
    dma = lambda *shape: pltpu.SemaphoreType.DMA(shape)
    vmem = pl.BlockSpec(memory_space=pltpu.VMEM)
    hbm = pl.BlockSpec(memory_space=pl.ANY)
    return pl.pallas_call(
        functools.partial(joint_kernel, tp_size, req_size),
        in_specs=[vmem] * 6 + [hbm] * 3,
        out_specs=[vmem, hbm],
        out_shape=[
            jax.ShapeDtypeStruct((rows, width), jnp.bfloat16),
            jax.ShapeDtypeStruct((req_size * tp_size, each, vocab), jnp.bfloat16),
        ],
        scratch_shapes=[
            pltpu.VMEM(mamba_out.shape, jnp.bfloat16),
            pltpu.VMEM(attention_out.shape, jnp.bfloat16),
            pltpu.VMEM((tp_size, rows, chunk), jnp.bfloat16),
            pltpu.VMEM((tp_size, rows, 128), jnp.float32),
            pltpu.VMEM((tp_size, rows, width), jnp.bfloat16),
            pltpu.VMEM((tp_size, rows, width), jnp.bfloat16),
            pltpu.VMEM((req_size, tp_size, rows, width), jnp.bfloat16),
            pltpu.VMEM((req_size * rows, model), jnp.bfloat16),
            pltpu.VMEM(output_head.shape, jnp.bfloat16),
            pltpu.VMEM((req_size, tp_size, each, vocab), jnp.bfloat16),
            dma(tp_size), dma(tp_size), dma(tp_size), dma(tp_size), dma(tp_size), dma(tp_size),
            dma(req_size, tp_size), dma(req_size, tp_size), dma(req_size, tp_size),
            dma(req_size, tp_size), dma(4),
        ],
        compiler_params=pltpu.CompilerParams(
            collective_id=1, has_side_effects=True, vmem_limit_bytes=60 << 20
        ),
    )(
        summed, stats, gated, mixer_gain[None], residual, final_gain[None], mamba_out, attention_out,
        output_head,
    )


def finish_kernel(residual_ref, blocks_ref, new_residual_ref, logits_ref):
    new_residual_ref[...] = residual_ref[...]
    width = blocks_ref.shape[2]
    for n in range(blocks_ref.shape[0]):
        logits_ref[:, n * width : (n + 1) * width] = blocks_ref[n].astype(jnp.float32)


def finish(residual, blocks):
    count, each, vocab = blocks.shape
    steps = 4
    part = count // steps
    return pl.pallas_call(
        finish_kernel,
        grid=(steps,),
        in_specs=[
            pl.BlockSpec(residual.shape, lambda i: (0, 0)),
            pl.BlockSpec((part, each, vocab), lambda i: (i, 0, 0)),
        ],
        out_specs=[
            pl.BlockSpec(residual.shape, lambda i: (0, 0)),
            pl.BlockSpec((each, part * vocab), lambda i: (0, i)),
        ],
        out_shape=[
            jax.ShapeDtypeStruct(residual.shape, residual.dtype),
            jax.ShapeDtypeStruct((each, count * vocab), jnp.float32),
        ],
    )(residual, blocks)


def body(
    residual,
    cache_lengths,
    input_gain,
    inner_weight,
    step_weight,
    step_bias,
    decay_log,
    skip_gain,
    conv_weight,
    conv_state,
    coupling_weight,
    coupling_conv,
    coupling_state,
    scan_state,
    mixer_gain,
    attention_weight,
    sink_cache,
    window_cache,
    mamba_out,
    attention_out,
    final_gain,
    output_head,
):
    row_count = residual.shape[0]
    tp_size = lax.axis_size("tp")
    local_units = inner_weight.shape[2]
    swap = lambda array: jnp.transpose(array, (1, 0, 2))
    coup_state = swap(coupling_state)
    normed, coupling_pre, qkv_rows, coupling_all, step_size, decay_rate = entry(
        step_bias, decay_log, residual, input_gain, attention_weight, coupling_weight,
        coupling_conv, coup_state, step_weight.T,
    )
    projected = jnp.einsum(
        "rd,dtc->trc", normed, inner_weight, preferred_element_type=jnp.float32
    ).astype(jnp.bfloat16)
    new_state, new_conv, new_coup, new_key_value, summed, stats, gated = mixer(
        cache_lengths, skip_gain, qkv_rows, sink_cache, window_cache,
        scan_state.reshape(row_count, local_units, NS), coupling_all, coupling_pre, coup_state,
        projected, conv_weight, swap(conv_state), step_size, decay_rate, tp_size,
    )
    new_conv_state = swap(new_conv)
    new_coupling_state = swap(new_coup)
    new_scan_state = new_state.reshape(scan_state.shape)
    fresh_residual, blocks = joint(
        summed, stats, gated, mixer_gain, mamba_out, attention_out, residual, final_gain, output_head
    )
    new_residual, logits = finish(fresh_residual, blocks)
    return (new_residual, logits, new_scan_state, new_conv_state, new_coupling_state, new_key_value)


def solution(mesh):
    return jax.shard_map(
        body,
        mesh=mesh,
        in_specs=(
            P("req", None),
            P("req"),
            P(),
            P(None, None, "tp"),
            P(None, "tp"),
            P("tp"),
            P("tp"),
            P("tp"),
            P(None, "tp"),
            P("req", None, "tp"),
            P(None, "tp"),
            P(None, "tp"),
            P("req", None, "tp"),
            P("req", "tp", None, None),
            P("tp"),
            P(None, "tp"),
            P("req", None, None),
            P("req", "tp", None),
            P("tp", None),
            P("tp", None),
            P(),
            P(None, ("req", "tp")),
        ),
        out_specs=(
            P("req", "tp"),
            P(("req", "tp"), None),
            P("req", "tp", None, None),
            P("req", None, "tp"),
            P("req", None, "tp"),
            P("req", None),
        ),
        check_vma=False,
    )
```

```python
import functools

import jax
import jax.numpy as jnp
from jax import lax
from jax.experimental import pallas as pl
from jax.experimental.pallas import tpu as pltpu
from jax.sharding import PartitionSpec as P

MH = 24
MP = 64
NS = 256
QH = 8
KVH = 2
HD = 128
WIN = 1024
SINK = 4
BR = 8

EPSILON = 1e-05
NEG_BIG = -1e30
MESH = pl.DeviceIdType.MESH
NT = (((1,), (1,)), ((), ()))


def norm_rows(values, gain):
    widened = values.astype(jnp.float32)
    mean_sq = jnp.mean(widened * widened, axis=-1, keepdims=True)
    return (widened * lax.rsqrt(mean_sq + EPSILON) * gain).astype(jnp.bfloat16)


def silu(v):
    return v / (1.0 + jnp.exp(-v))


def conv_rows(old, fresh, taps_ref):
    steps = [row.astype(jnp.float32) for row in (*old, fresh)]
    taps = taps_ref[...].astype(jnp.float32)
    mixed = steps[0] * taps[0:1]
    for k in range(1, 4):
        mixed = mixed + steps[k] * taps[k : k + 1]
    return silu(mixed)


def by_head(ref, g, shape):
    lane = lax.broadcasted_iota(jnp.int32, shape, 1)
    return jnp.where(lane < MP, ref[2 * g], ref[2 * g + 1])


def entry_kernel(
    tp_size, bias_src, log_src, residual_src, gain_src, attention_src, coupling_src, taps_src,
    state_src, step_weight_src, normed_ref, pre_ref, qkv_ref, coup_ref, step_ref, decay_ref,
    residual_ref, gain_ref, attention_ref, coupling_ref, taps_ref,
    state_ref, step_weight_ref, bias_ref, log_ref, load_sem, qkv_s, qkv_r, coup_s, coup_r,
):
    r = lax.axis_index("req")
    t = lax.axis_index("tp")
    peers = [lax.rem(t + k, tp_size) for k in range(tp_size)]
    barrier = pltpu.get_barrier_semaphore()
    for k in range(1, tp_size):
        pl.semaphore_signal(barrier, inc=1, device_id=(r, peers[k]), device_id_type=MESH)
    sources = [
        residual_src, gain_src, attention_src, coupling_src, taps_src, state_src, step_weight_src,
        bias_src, log_src,
    ]
    places = [
        residual_ref, gain_ref, attention_ref, coupling_ref, taps_ref, state_ref, step_weight_ref,
        bias_ref, log_ref,
    ]
    loads = [
        pltpu.make_async_copy(src, dst, load_sem.at[n])
        for n, (src, dst) in enumerate(zip(sources, places))
    ]
    for load in loads:
        load.start()
    loads[0].wait()
    loads[1].wait()
    normed = norm_rows(residual_ref[...], gain_ref[...])
    normed_ref[...] = normed
    copies = []

    def share(out_ref, value, ssem, rsem):
        width = value.shape[1]
        cols = pl.ds(pl.multiple_of(t * width, 128), width)
        out_ref[:, cols] = value
        for k in range(1, tp_size):
            copy = pltpu.make_async_remote_copy(
                src_ref=out_ref.at[:, cols], dst_ref=out_ref.at[:, cols], send_sem=ssem.at[k],
                recv_sem=rsem.at[k], device_id=(r, peers[k]), device_id_type=MESH,
            )
            copy.start()
            copies.append(copy)

    loads[2].wait()
    qkv = jnp.dot(normed, attention_ref[...], preferred_element_type=jnp.float32)
    pl.semaphore_wait(barrier, tp_size - 1)
    share(qkv_ref, qkv.astype(jnp.bfloat16), qkv_s, qkv_r)
    for load in loads[3:]:
        load.wait()
    pre = jnp.dot(normed, coupling_ref[...], preferred_element_type=jnp.float32).astype(jnp.bfloat16)
    pre_ref[...] = pre
    share(coup_ref, conv_rows([state_ref[k] for k in range(3)], pre, taps_ref).astype(jnp.bfloat16), coup_s, coup_r)
    steps = (
        lax.dot_general(normed, step_weight_ref[...], NT, preferred_element_type=jnp.float32)
        .astype(jnp.bfloat16)
        .astype(jnp.float32)
    )
    shape = (normed.shape[0], 2 * MP)
    for g in range(steps.shape[1] // 2):
        lane = lax.broadcasted_iota(jnp.int32, shape, 1)
        v = jnp.where(lane < MP, steps[:, 2 * g : 2 * g + 1], steps[:, 2 * g + 1 : 2 * g + 2])
        v = v + by_head(bias_ref, g, shape)
        size = jnp.maximum(v, 0.0) + jnp.log1p(jnp.exp(-jnp.abs(v)))
        step_ref[:, g * 2 * MP : (g + 1) * 2 * MP] = size
        decay_ref[:, g * 2 * MP : (g + 1) * 2 * MP] = jnp.exp(
            -size * jnp.exp(by_head(log_ref, g, shape))
        )
    for copy in copies:
        copy.wait()


def entry(bias, decay_log, residual, gain, attention_weight, coupling_weight, taps, state, step_weight):
    tp_size = lax.axis_size("tp")
    rows, model = residual.shape
    units = bias.shape[0] * MP
    vmem = pl.BlockSpec(memory_space=pltpu.VMEM)
    hbm = pl.BlockSpec(memory_space=pltpu.HBM)
    dma = pltpu.SemaphoreType.DMA((tp_size,))
    operands = (residual, gain[None], attention_weight, coupling_weight, taps, state, step_weight)
    levels = (bias, decay_log)
    shaped = jax.ShapeDtypeStruct
    keep = lambda a: pltpu.with_memory_space_constraint(a, pltpu.HBM)
    return pl.pallas_call(
        functools.partial(entry_kernel, tp_size),
        in_specs=[hbm] * 9,
        out_specs=[vmem] * 6,
        out_shape=[
            shaped((rows, model), jnp.bfloat16),
            shaped((rows, coupling_weight.shape[1]), jnp.bfloat16),
            shaped((rows, attention_weight.shape[1] * tp_size), jnp.bfloat16),
            shaped((rows, coupling_weight.shape[1] * tp_size), jnp.bfloat16),
            shaped((rows, units), jnp.float32),
            shaped((rows, units), jnp.float32),
        ],
        scratch_shapes=[pltpu.VMEM(a.shape, a.dtype) for a in operands]
        + [pltpu.SMEM(a.shape, a.dtype) for a in levels]
        + [pltpu.SemaphoreType.DMA((len(operands) + len(levels),))]
        + [dma] * 4,
        cost_estimate=pl.CostEstimate(flops=9_000_000_000, bytes_accessed=3_000_000, transcendentals=0),
        compiler_params=pltpu.CompilerParams(
            collective_id=0, has_side_effects=True, vmem_limit_bytes=8 << 20
        ),
    )(*map(keep, levels), *map(keep, operands))


def mixer_kernel(
    len_ref, skip_ref, qkv_ref, sink_ref, window_ref, state_ref, coup_ref, pre_ref, coup_state_ref,
    projected_ref, taps_ref, conv_state_ref, step_ref, decay_ref, new_state_ref, new_conv_ref,
    new_coup_ref, key_value_ref, summed_ref, stats_ref, gated_ref, heads_scr, stat_scr, extra_scr,
):
    half = KVH * HD
    group = QH // KVH
    i = pl.program_id(0)
    t = lax.axis_index("tp")
    units = step_ref.shape[2]
    slots = window_ref.shape[1]
    coup = coup_ref[i]
    out_rows = coup[:, NS:]
    in_f32 = coup[:, :NS].astype(jnp.float32)
    qkv = qkv_ref[i]
    fresh = qkv[:, QH * HD :]
    key_value_ref[i] = fresh

    for h in range(QH):
        heads_scr[pl.ds(h, BR, stride=QH), :] = qkv[:, h * HD : (h + 1) * HD].astype(jnp.float32)
    for j in range(BR):
        extra_scr[j * SINK : (j + 1) * SINK, :] = sink_ref[i * BR + j].astype(jnp.float32)
    extra_scr[BR * SINK : BR * SINK + BR, :] = fresh.astype(jnp.float32)
    extra_scr[BR * SINK + BR :, :] = jnp.zeros_like(extra_scr[BR * SINK + BR :, :])
    extra = extra_scr[...].astype(jnp.bfloat16)
    head_row = lax.broadcasted_iota(jnp.int32, (BR * QH, HD), 0) % QH
    lane = lax.broadcasted_iota(jnp.int32, (BR * QH, HD), 1)
    first_half = head_row < group
    q = heads_scr[...]
    wide = jnp.concatenate([jnp.where(first_half, q, 0.0), jnp.where(first_half, 0.0, q)], axis=1)
    block = lambda array, j: array[j * QH : (j + 1) * QH]
    slot = t * slots + lax.broadcasted_iota(jnp.int32, (QH, slots), 1)
    lives, scores = [], []
    for j in range(BR):
        last = len_ref[i * BR + j] - 1
        back = jnp.bitwise_and(last - slot, WIN - 1)
        lives.append((last - back >= SINK) & (back != WIN - 1))
        raw = lax.dot_general(
            block(wide, j).astype(jnp.bfloat16), window_ref[j, :, :half], NT,
            preferred_element_type=jnp.float32,
        )
        scores.append(jnp.where(lives[j], raw * HD ** (-0.5), NEG_BIG))
    s1 = jnp.concatenate(scores, axis=0)
    s2 = lax.dot_general(
        wide.astype(jnp.bfloat16), extra[:, :half], NT, preferred_element_type=jnp.float32
    ) * HD ** (-0.5)
    col = lax.broadcasted_iota(jnp.int32, s2.shape, 1)
    owner = lax.broadcasted_iota(jnp.int32, s2.shape, 0) // QH
    live2 = (jnp.where(col < BR * SINK, col // SINK, col - BR * SINK) == owner) & (t == 0)
    s2 = jnp.where(live2, s2, NEG_BIG)
    peak = jnp.maximum(jnp.max(s1, axis=1, keepdims=True), jnp.max(s2, axis=1, keepdims=True))
    w1 = jnp.exp(s1 - peak)
    w1 = jnp.concatenate([jnp.where(lives[j], block(w1, j), 0.0) for j in range(BR)], axis=0)
    w2 = jnp.where(live2, jnp.exp(s2 - peak), 0.0)
    total = jnp.sum(w1, axis=1, keepdims=True) + jnp.sum(w2, axis=1, keepdims=True)
    acc = jnp.concatenate(
        [
            jnp.dot(
                block(w1, j).astype(jnp.bfloat16), window_ref[j, :, half:],
                preferred_element_type=jnp.float32,
            )
            for j in range(BR)
        ],
        axis=0,
    ) + jnp.dot(w2.astype(jnp.bfloat16), extra[:, half:], preferred_element_type=jnp.float32)
    heads_scr[...] = jnp.where(first_half, acc[:, :HD], acc[:, HD:])
    stat_scr[...] = jnp.where(lane == head_row, peak, 0.0) + jnp.where(
        lane == head_row + QH, total, 0.0
    )
    stats = functools.reduce(jnp.add, [stat_scr[pl.ds(h, BR, stride=QH), :] for h in range(QH)])
    per_chunk = summed_ref.shape[3] // HD
    for h in range(QH):
        summed_ref[h // per_chunk, i, :, (h % per_chunk) * HD : (h % per_chunk + 1) * HD] = heads_scr[
            pl.ds(h, BR, stride=QH), :
        ].astype(jnp.bfloat16)

    gate = projected_ref[0, i].astype(jnp.float32)
    x_pre = projected_ref[1, i]
    x = conv_rows([conv_state_ref[k, i] for k in range(3)], x_pre, taps_ref)
    new_conv_ref[0, i] = conv_state_ref[1, i]
    new_conv_ref[1, i] = conv_state_ref[2, i]
    new_conv_ref[2, i] = x_pre
    new_coup_ref[0, i] = coup_state_ref[1, i]
    new_coup_ref[1, i] = coup_state_ref[2, i]
    new_coup_ref[2, i] = pre_ref[i]
    step_x = step_ref[i] * x
    decay = decay_ref[i]
    both = jnp.sum(in_f32 * out_rows.astype(jnp.float32), axis=1, keepdims=True)
    step_x_t = step_x.T
    decay_t = decay.T
    read_rows = []
    for j in range(BR):
        state = state_ref[j]
        read_rows.append(
            lax.dot_general(out_rows, state, NT, preferred_element_type=jnp.float32)[j : j + 1, :]
        )
        new_state_ref[j] = (
            decay_t[:, j : j + 1] * state.astype(jnp.float32)
            + step_x_t[:, j : j + 1] * in_f32[j : j + 1, :]
        ).astype(jnp.bfloat16)
    readout = decay * jnp.concatenate(read_rows, axis=0) + step_x * both
    skip = jnp.concatenate(
        [by_head(skip_ref, g, (BR, 2 * MP)) for g in range(units // (2 * MP))], axis=1
    )
    gated = (readout + skip * x) * silu(gate)
    gated_ref[i] = gated
    square = jnp.sum(gated * gated, axis=1, keepdims=True)
    stats_ref[i] = jnp.where(
        lax.broadcasted_iota(jnp.int32, stats.shape, 1) == 2 * QH, square, stats
    )


def mixer(
    lengths, skip, qkv, sink, window, state, coup, pre, coup_state, projected, taps, conv_state,
    step, decay, tp_size,
):
    rows, units = step.shape
    blocks = rows // BR

    def split(a):
        at = a.ndim - 2
        return a.reshape(a.shape[:at] + (blocks, BR) + a.shape[at + 1 :])

    whole = lambda shape: pl.BlockSpec(shape, lambda i: (0,) * len(shape))
    cube = lambda a: pl.BlockSpec((BR,) + a.shape[1:], lambda i: (i, 0, 0))
    smem = pl.BlockSpec(memory_space=pltpu.SMEM)
    chunk = QH * HD // tp_size
    small = [split(a) for a in (coup, pre, coup_state, projected)]
    late = [split(a) for a in (conv_state, step, decay)]
    qkv = split(qkv)
    outs = [
        ((3, blocks, BR, units), jnp.bfloat16),
        ((3, blocks, BR, coup_state.shape[2]), jnp.bfloat16),
        ((blocks, BR, 2 * KVH * HD), jnp.bfloat16),
        ((tp_size, blocks, BR, chunk), jnp.bfloat16),
        ((blocks, BR, 128), jnp.float32),
        ((blocks, BR, units), jnp.float32),
    ]
    results = pl.pallas_call(
        mixer_kernel,
        grid=(blocks,),
        in_specs=[smem, smem, whole(qkv.shape), whole(sink.shape), cube(window), cube(state)]
        + [whole(a.shape) for a in small]
        + [whole(taps.shape)]
        + [whole(a.shape) for a in late],
        out_specs=[cube(state)] + [whole(shape) for shape, _ in outs],
        out_shape=[jax.ShapeDtypeStruct(state.shape, jnp.bfloat16)]
        + [jax.ShapeDtypeStruct(shape, kind) for shape, kind in outs],
        scratch_shapes=[
            pltpu.VMEM((BR * QH, HD), jnp.float32),
            pltpu.VMEM((BR * QH, HD), jnp.float32),
            pltpu.VMEM((BR * QH, 2 * KVH * HD), jnp.float32),
        ],
        cost_estimate=pl.CostEstimate(flops=1_000_000_000, bytes_accessed=21_000_000, transcendentals=0),
        compiler_params=pltpu.CompilerParams(vmem_limit_bytes=16 << 20),
    )(lengths, skip, qkv, sink, window, state, *small, taps, *late)
    merge = lambda a: a.reshape(a.shape[:-3] + (rows, a.shape[-1]))
    return [results[0]] + [merge(a) for a in results[1:]]


def other(index, k):
    bit = 1
    while bit <= k:
        if k & bit:
            index = index + bit - 2 * bit * lax.rem(lax.div(index, bit), 2)
        bit *= 2
    return index


def joint_kernel(
    tp_size, req_size, summed_ref, stats_ref, gated_ref, mixer_gain_ref, residual_ref, final_gain_ref,
    mamba_out_ref, attention_out_ref, head_ref, new_residual_ref, logits_ref, mamba_buf, attention_buf,
    sum_buf, stat_buf, part_out, part_buf, gather, final_buf, head_buf, logit_out,
    sum_s, sum_r, stat_s, stat_r, part_s, part_r, gat_s, gat_r, log_s, log_r, load_sem,
):
    r = lax.axis_index("req")
    t = lax.axis_index("tp")
    rows = gated_ref.shape[0]
    width = new_residual_ref.shape[1]
    peers = [other(t, q) for q in range(tp_size)]
    reqs = [other(r, k) for k in range(req_size)]
    barrier = pltpu.get_barrier_semaphore()
    for q in range(1, tp_size):
        pl.semaphore_signal(barrier, inc=1, device_id=(r, peers[q]), device_id_type=MESH)
    for k in range(1, req_size):
        pl.semaphore_signal(barrier, inc=1, device_id=(reqs[k], t), device_id_type=MESH)
    loads = [
        pltpu.make_async_copy(src, dst, load_sem.at[n])
        for n, (src, dst) in enumerate(
            [(mamba_out_ref, mamba_buf), (attention_out_ref, attention_buf), (head_ref, head_buf)]
        )
    ]
    for load in loads:
        load.start()
    pl.semaphore_wait(barrier, tp_size + req_size - 2)

    def send(src, dst, ssem, rsem, where):
        copy = pltpu.make_async_remote_copy(
            src_ref=src, dst_ref=dst, send_sem=ssem, recv_sem=rsem,
            device_id=where, device_id_type=MESH,
        )
        copy.start()
        return copy

    first = []
    for q in reversed(range(1, tp_size)):
        where = (r, peers[q])
        first.append(send(stats_ref, stat_buf.at[q], stat_s.at[q], stat_r.at[q], where))
        first.append(send(summed_ref.at[peers[q]], sum_buf.at[q], sum_s.at[q], sum_r.at[q], where))
    mamba = (gated_ref[...] * mixer_gain_ref[...][None]).astype(jnp.bfloat16)
    columns = lambda p: pl.ds(pl.multiple_of(p * width, 128), width)
    loads[0].wait()
    unscaled = [
        jnp.dot(mamba, mamba_buf[:, columns(peers[q])], preferred_element_type=jnp.float32)
        for q in range(tp_size)
    ]
    loads[1].wait()
    for copy in first:
        copy.wait()
    stats = [stats_ref[...]] + [stat_buf[q] for q in range(1, tp_size)]
    sums = [summed_ref[t].astype(jnp.float32)] + [
        sum_buf[q].astype(jnp.float32) for q in range(1, tp_size)
    ]
    lane = lax.broadcasted_iota(jnp.int32, (rows, 128), 1)
    local_heads = QH // tp_size
    pieces = []
    for hl in range(local_heads):
        h = t * local_heads + hl
        peaks = [jnp.sum(jnp.where(lane == h, s, 0.0), axis=1, keepdims=True) for s in stats]
        totals = [jnp.sum(jnp.where(lane == h + QH, s, 0.0), axis=1, keepdims=True) for s in stats]
        top = functools.reduce(jnp.maximum, peaks)
        scales = [jnp.exp(p - top) for p in peaks]
        below = functools.reduce(jnp.add, [a * b for a, b in zip(scales, totals)])
        above = functools.reduce(
            jnp.add, [a * b[:, hl * HD : (hl + 1) * HD] for a, b in zip(scales, sums)]
        )
        pieces.append((above / below).astype(jnp.bfloat16))
    attended = jnp.concatenate(pieces, axis=1)
    square = functools.reduce(jnp.add, [s[:, 2 * QH : 2 * QH + 1] for s in stats])
    mamba_scale = lax.rsqrt(square / (MH * MP) + EPSILON)

    def partial(q):
        return mamba_scale * unscaled[q] + jnp.dot(
            attended, attention_buf[:, columns(peers[q])], preferred_element_type=jnp.float32
        )

    second = {}
    for q in reversed(range(1, tp_size)):
        part_out[q] = partial(q).astype(jnp.bfloat16)
        second[q] = send(part_out.at[q], part_buf.at[q], part_s.at[q], part_r.at[q], (r, peers[q]))
    mixed = residual_ref[:, columns(t)].astype(jnp.float32) + partial(0)
    for q in range(1, tp_size):
        second[q].wait()
        mixed = mixed + part_buf[q].astype(jnp.float32)
    fresh = mixed.astype(jnp.bfloat16)
    new_residual_ref[...] = fresh
    gather[0, 0] = fresh

    half = req_size // 2
    far_groups = list(range(half, req_size))
    near_groups = list(range(2, half)) + [1]
    along, over, near, far = {}, {}, {}, {}
    for k in far_groups + near_groups:
        along[k] = send(
            gather.at[0, 0], gather.at[k, 0], gat_s.at[k, 0], gat_r.at[k, 0], (reqs[k], t)
        )

    def spread(k):
        if k:
            along[k].wait_recv()
        over[k] = send(
            gather.at[k, 0], gather.at[k, 2], gat_s.at[k, 2], gat_r.at[k, 2], (r, peers[2])
        )
        near[k] = send(
            gather.at[k, 0], gather.at[k, 1], gat_s.at[k, 1], gat_r.at[k, 1], (r, peers[1])
        )

    def pair_up(k):
        over[k].wait_recv()
        far[k] = send(
            gather.at[k, 2], gather.at[k, 3], gat_s.at[k, 3], gat_r.at[k, 3], (r, peers[1])
        )

    vocab = head_buf.shape[1]
    tile = min(512, vocab)
    each = rows // tp_size
    source = r * tp_size + t
    sent = []

    def project(groups):
        for k in groups:
            near[k].wait_recv()
            far[k].wait_recv()
            values = [gather[k, i].astype(jnp.float32) for i in range(tp_size)]
            mean = functools.reduce(
                jnp.add, [jnp.sum(v * v, axis=1, keepdims=True) for v in values]
            ) / (width * tp_size)
            scale = lax.rsqrt(mean + EPSILON)
            for i in range(tp_size):
                cols = columns(peers[i])
                final_buf[k * rows : (k + 1) * rows, cols] = (
                    values[i] * scale * final_gain_ref[:, cols]
                ).astype(jnp.bfloat16)
        low = groups[0] * rows
        high = low + len(groups) * rows

        def head_tile(c, carry):
            cols = pl.ds(pl.multiple_of(c * tile, 128), tile)
            part = jnp.dot(
                final_buf[low:high, :], head_buf[:, cols], preferred_element_type=jnp.float32
            )
            for n, k in enumerate(groups):
                for q in range(tp_size):
                    at = n * rows + q * each
                    logit_out[k, q, :, cols] = part[at : at + each, :].astype(jnp.bfloat16)
            return carry

        lax.fori_loop(0, vocab // tile, head_tile, 0)
        for k in groups:
            for q in reversed(range(tp_size)):
                if k or q:
                    sent.append(
                        send(
                            logit_out.at[k, peers[q]], logits_ref.at[source], log_s.at[k, q],
                            log_r.at[k, q], (reqs[k], peers[q]),
                        )
                    )

    early, rest = far_groups[:2], far_groups[2:]
    spread(0)
    for k in early:
        spread(k)
    pair_up(0)
    loads[2].wait()
    project([0])
    own = pltpu.make_async_copy(logit_out.at[0, t], logits_ref.at[source], load_sem.at[3])
    own.start()
    for k in rest + near_groups:
        spread(k)
    for k in early:
        pair_up(k)
    for n, k in enumerate(early):
        project([k])
        if n == 0:
            for later in rest:
                pair_up(later)
    for k in near_groups:
        pair_up(k)
    for k in rest[::2]:
        project([k, k + 1])
    for k in near_groups[:-1:2]:
        project([k, k + 1])
    project([1])
    own.wait()
    for copy in sent:
        copy.wait()
    for copies in (along, over, near, far):
        for copy in copies.values():
            copy.wait_send()


def joint(
    summed, stats, gated, mixer_gain, mamba_out, attention_out, residual, final_gain, output_head
):
    tp_size = lax.axis_size("tp")
    req_size = lax.axis_size("req")
    rows, model = residual.shape
    width = model // tp_size
    chunk = summed.shape[2]
    each = rows // tp_size
    vocab = output_head.shape[1]
    dma = lambda *shape: pltpu.SemaphoreType.DMA(shape)
    vmem = pl.BlockSpec(memory_space=pltpu.VMEM)
    hbm = pl.BlockSpec(memory_space=pl.ANY)
    return pl.pallas_call(
        functools.partial(joint_kernel, tp_size, req_size),
        in_specs=[vmem] * 6 + [hbm] * 3,
        out_specs=[vmem, pl.BlockSpec(memory_space=pltpu.HBM)],
        out_shape=[
            jax.ShapeDtypeStruct((rows, width), jnp.bfloat16),
            jax.ShapeDtypeStruct((req_size * tp_size, each, vocab), jnp.bfloat16),
        ],
        scratch_shapes=[
            pltpu.VMEM(mamba_out.shape, jnp.bfloat16),
            pltpu.VMEM(attention_out.shape, jnp.bfloat16),
            pltpu.VMEM((tp_size, rows, chunk), jnp.bfloat16),
            pltpu.VMEM((tp_size, rows, 128), jnp.float32),
            pltpu.VMEM((tp_size, rows, width), jnp.bfloat16),
            pltpu.VMEM((tp_size, rows, width), jnp.bfloat16),
            pltpu.VMEM((req_size, tp_size, rows, width), jnp.bfloat16),
            pltpu.VMEM((req_size * rows, model), jnp.bfloat16),
            pltpu.VMEM(output_head.shape, jnp.bfloat16),
            pltpu.VMEM((req_size, tp_size, each, vocab), jnp.bfloat16),
            dma(tp_size), dma(tp_size), dma(tp_size), dma(tp_size), dma(tp_size), dma(tp_size),
            dma(req_size, tp_size), dma(req_size, tp_size), dma(req_size, tp_size),
            dma(req_size, tp_size), dma(4),
        ],
        cost_estimate=pl.CostEstimate(flops=40_000_000_000, bytes_accessed=12_000_000, transcendentals=0),
        compiler_params=pltpu.CompilerParams(
            collective_id=1, has_side_effects=True, vmem_limit_bytes=24 << 20
        ),
    )(
        summed, stats, gated, mixer_gain, residual, final_gain[None], mamba_out, attention_out,
        output_head,
    )


def finish_kernel(residual_ref, blocks_ref, new_residual_ref, logits_ref):
    new_residual_ref[...] = residual_ref[...]
    width = blocks_ref.shape[2]
    for n in range(blocks_ref.shape[0]):
        logits_ref[:, n * width : (n + 1) * width] = blocks_ref[n].astype(jnp.float32)


def finish(residual, blocks):
    count, each, vocab = blocks.shape
    steps = 4
    part = count // steps
    return pl.pallas_call(
        finish_kernel,
        grid=(steps,),
        in_specs=[
            pl.BlockSpec(residual.shape, lambda i: (0, 0)),
            pl.BlockSpec((part, each, vocab), lambda i: (i, 0, 0)),
        ],
        out_specs=[
            pl.BlockSpec(residual.shape, lambda i: (0, 0)),
            pl.BlockSpec((each, part * vocab), lambda i: (0, i)),
        ],
        out_shape=[
            jax.ShapeDtypeStruct(residual.shape, residual.dtype),
            jax.ShapeDtypeStruct((each, count * vocab), jnp.float32),
        ],
        compiler_params=pltpu.CompilerParams(vmem_limit_bytes=8 << 20),
    )(residual, blocks)


def body(
    residual,
    cache_lengths,
    input_gain,
    inner_weight,
    step_weight,
    step_bias,
    decay_log,
    skip_gain,
    conv_weight,
    conv_state,
    coupling_weight,
    coupling_conv,
    coupling_state,
    scan_state,
    mixer_gain,
    attention_weight,
    sink_cache,
    window_cache,
    mamba_out,
    attention_out,
    final_gain,
    output_head,
):
    row_count = residual.shape[0]
    tp_size = lax.axis_size("tp")
    local_units = inner_weight.shape[2]
    swap = lambda array: jnp.transpose(array, (1, 0, 2))
    coup_state = swap(coupling_state)
    normed, coupling_pre, qkv_rows, coupling_all, step_size, decay_rate = entry(
        step_bias, decay_log, residual, input_gain, attention_weight, coupling_weight,
        coupling_conv, coup_state, step_weight.T,
    )
    projected = jnp.einsum(
        "rd,dtc->trc", normed, inner_weight, preferred_element_type=jnp.float32
    ).astype(jnp.bfloat16)
    new_state, new_conv, new_coup, new_key_value, summed, stats, gated = mixer(
        cache_lengths, skip_gain, qkv_rows, sink_cache, window_cache,
        scan_state.reshape(row_count, local_units, NS), coupling_all, coupling_pre, coup_state,
        projected, conv_weight, swap(conv_state), step_size, decay_rate, tp_size,
    )
    new_conv_state = swap(new_conv)
    new_coupling_state = swap(new_coup)
    new_scan_state = new_state.reshape(scan_state.shape)
    fresh_residual, blocks = joint(
        summed, stats, gated, mixer_gain, mamba_out, attention_out, residual, final_gain, output_head
    )
    new_residual, logits = finish(fresh_residual, blocks)
    return (new_residual, logits, new_scan_state, new_conv_state, new_coupling_state, new_key_value)


def solution(mesh):
    return jax.shard_map(
        body,
        mesh=mesh,
        in_specs=(
            P("req", None),
            P("req"),
            P(),
            P(None, None, "tp"),
            P(None, "tp"),
            P("tp"),
            P("tp"),
            P("tp"),
            P(None, "tp"),
            P("req", None, "tp"),
            P(None, "tp"),
            P(None, "tp"),
            P("req", None, "tp"),
            P("req", "tp", None, None),
            P("tp"),
            P(None, "tp"),
            P("req", None, None),
            P("req", "tp", None),
            P("tp", None),
            P("tp", None),
            P(),
            P(None, ("req", "tp")),
        ),
        out_specs=(
            P("req", "tp"),
            P(("req", "tp"), None),
            P("req", "tp", None, None),
            P("req", None, "tp"),
            P("req", None, "tp"),
            P("req", None),
        ),
        check_vma=False,
    )
```

```python
import functools

import jax
import jax.numpy as jnp
from jax import lax
from jax.experimental import pallas as pl
from jax.experimental.pallas import tpu as pltpu
from jax.sharding import PartitionSpec as P

MH = 24
MP = 64
NS = 256
QH = 8
KVH = 2
HD = 128
WIN = 1024
SINK = 4
BR = 8

EPSILON = 1e-05
NEG_BIG = -1e30
MESH = pl.DeviceIdType.MESH
NT = (((1,), (1,)), ((), ()))


def norm_rows(values, gain):
    widened = values.astype(jnp.float32)
    mean_sq = jnp.mean(widened * widened, axis=-1, keepdims=True)
    return (widened * lax.rsqrt(mean_sq + EPSILON) * gain).astype(jnp.bfloat16)


def silu(v):
    return v / (1.0 + jnp.exp(-v))


def conv_rows(old, fresh, taps_ref):
    steps = [row.astype(jnp.float32) for row in (*old, fresh)]
    taps = taps_ref[...].astype(jnp.float32)
    mixed = steps[0] * taps[0:1]
    for k in range(1, 4):
        mixed = mixed + steps[k] * taps[k : k + 1]
    return silu(mixed)


def by_head(ref, g, shape):
    lane = lax.broadcasted_iota(jnp.int32, shape, 1)
    return jnp.where(lane < MP, ref[2 * g], ref[2 * g + 1])


def entry_kernel(
    tp_size, bias_src, log_src, residual_src, gain_src, attention_src, coupling_src, taps_src,
    state_src, step_weight_src, normed_ref, pre_ref, qkv_ref, coup_ref, step_ref, decay_ref,
    residual_ref, gain_ref, attention_ref, coupling_ref, taps_ref,
    state_ref, step_weight_ref, bias_ref, log_ref, load_sem, qkv_s, qkv_r, coup_s, coup_r,
):
    r = lax.axis_index("req")
    t = lax.axis_index("tp")
    peers = [lax.rem(t + k, tp_size) for k in range(tp_size)]
    barrier = pltpu.get_barrier_semaphore()
    for k in range(1, tp_size):
        pl.semaphore_signal(barrier, inc=1, device_id=(r, peers[k]), device_id_type=MESH)
    sources = [
        residual_src, gain_src, attention_src, coupling_src, taps_src, state_src, step_weight_src,
        bias_src, log_src,
    ]
    places = [
        residual_ref, gain_ref, attention_ref, coupling_ref, taps_ref, state_ref, step_weight_ref,
        bias_ref, log_ref,
    ]
    loads = [
        pltpu.make_async_copy(src, dst, load_sem.at[n])
        for n, (src, dst) in enumerate(zip(sources, places))
    ]
    for load in loads:
        load.start()
    loads[0].wait()
    loads[1].wait()
    normed = norm_rows(residual_ref[...], gain_ref[...])
    normed_ref[...] = normed
    copies = []

    def share(out_ref, value, ssem, rsem):
        width = value.shape[1]
        cols = pl.ds(pl.multiple_of(t * width, 128), width)
        out_ref[:, cols] = value
        for k in range(1, tp_size):
            copy = pltpu.make_async_remote_copy(
                src_ref=out_ref.at[:, cols], dst_ref=out_ref.at[:, cols], send_sem=ssem.at[k],
                recv_sem=rsem.at[k], device_id=(r, peers[k]), device_id_type=MESH,
            )
            copy.start()
            copies.append(copy)

    loads[2].wait()
    qkv = jnp.dot(normed, attention_ref[...], preferred_element_type=jnp.float32)
    pl.semaphore_wait(barrier, tp_size - 1)
    share(qkv_ref, qkv.astype(jnp.bfloat16), qkv_s, qkv_r)
    for load in loads[3:]:
        load.wait()
    pre = jnp.dot(normed, coupling_ref[...], preferred_element_type=jnp.float32).astype(jnp.bfloat16)
    pre_ref[...] = pre
    share(coup_ref, conv_rows([state_ref[k] for k in range(3)], pre, taps_ref).astype(jnp.bfloat16), coup_s, coup_r)
    steps = (
        lax.dot_general(normed, step_weight_ref[...], NT, preferred_element_type=jnp.float32)
        .astype(jnp.bfloat16)
        .astype(jnp.float32)
    )
    shape = (normed.shape[0], 2 * MP)
    for g in range(steps.shape[1] // 2):
        lane = lax.broadcasted_iota(jnp.int32, shape, 1)
        v = jnp.where(lane < MP, steps[:, 2 * g : 2 * g + 1], steps[:, 2 * g + 1 : 2 * g + 2])
        v = v + by_head(bias_ref, g, shape)
        size = jnp.maximum(v, 0.0) + jnp.log1p(jnp.exp(-jnp.abs(v)))
        step_ref[:, g * 2 * MP : (g + 1) * 2 * MP] = size
        decay_ref[:, g * 2 * MP : (g + 1) * 2 * MP] = jnp.exp(
            -size * jnp.exp(by_head(log_ref, g, shape))
        )
    for copy in copies:
        copy.wait()


def entry(bias, decay_log, residual, gain, attention_weight, coupling_weight, taps, state, step_weight):
    tp_size = lax.axis_size("tp")
    rows, model = residual.shape
    units = bias.shape[0] * MP
    vmem = pl.BlockSpec(memory_space=pltpu.VMEM)
    hbm = pl.BlockSpec(memory_space=pltpu.HBM)
    dma = pltpu.SemaphoreType.DMA((tp_size,))
    operands = (residual, gain[None], attention_weight, coupling_weight, taps, state, step_weight)
    levels = (bias, decay_log)
    shaped = jax.ShapeDtypeStruct
    return pl.pallas_call(
        functools.partial(entry_kernel, tp_size),
        in_specs=[hbm] * 9,
        out_specs=[vmem] * 6,
        out_shape=[
            shaped((rows, model), jnp.bfloat16),
            shaped((rows, coupling_weight.shape[1]), jnp.bfloat16),
            shaped((rows, attention_weight.shape[1] * tp_size), jnp.bfloat16),
            shaped((rows, coupling_weight.shape[1] * tp_size), jnp.bfloat16),
            shaped((rows, units), jnp.float32),
            shaped((rows, units), jnp.float32),
        ],
        scratch_shapes=[pltpu.VMEM(a.shape, a.dtype) for a in operands]
        + [pltpu.SMEM(a.shape, a.dtype) for a in levels]
        + [pltpu.SemaphoreType.DMA((len(operands) + len(levels),))]
        + [dma] * 4,
        cost_estimate=pl.CostEstimate(flops=9_000_000_000, bytes_accessed=3_000_000, transcendentals=0),
        compiler_params=pltpu.CompilerParams(
            collective_id=0, has_side_effects=True, vmem_limit_bytes=8 << 20
        ),
    )(*map(keep, levels), *map(keep, operands))


def mix_block(
    i, len_ref, skip_ref, qkv_ref, sink_ref, window_ref, state_ref, coup_ref, projected_ref, taps_ref,
    conv_state_ref, step_ref, decay_ref, summed_ref, stats_ref, gated_ref, step_x_ref, heads_scr,
    stat_scr, extra_scr,
):
    half = KVH * HD
    group = QH // KVH
    t = lax.axis_index("tp")
    units = step_ref.shape[2]
    slots = window_ref.shape[1]
    coup = coup_ref[i]
    out_rows = coup[:, NS:]
    in_f32 = coup[:, :NS].astype(jnp.float32)
    qkv = qkv_ref[i]
    fresh = qkv[:, QH * HD :]

    for h in range(QH):
        heads_scr[pl.ds(h, BR, stride=QH), :] = qkv[:, h * HD : (h + 1) * HD].astype(jnp.float32)
    for j in range(BR):
        extra_scr[j * SINK : (j + 1) * SINK, :] = sink_ref[i * BR + j].astype(jnp.float32)
    extra_scr[BR * SINK : BR * SINK + BR, :] = fresh.astype(jnp.float32)
    extra_scr[BR * SINK + BR :, :] = jnp.zeros_like(extra_scr[BR * SINK + BR :, :])
    extra = extra_scr[...].astype(jnp.bfloat16)
    head_row = lax.broadcasted_iota(jnp.int32, (BR * QH, HD), 0) % QH
    lane = lax.broadcasted_iota(jnp.int32, (BR * QH, HD), 1)
    first_half = head_row < group
    q = heads_scr[...]
    wide = jnp.concatenate([jnp.where(first_half, q, 0.0), jnp.where(first_half, 0.0, q)], axis=1)
    block = lambda array, j: array[j * QH : (j + 1) * QH]
    slot = t * slots + lax.broadcasted_iota(jnp.int32, (QH, slots), 1)
    lives, scores = [], []
    for j in range(BR):
        last = len_ref[i * BR + j] - 1
        back = jnp.bitwise_and(last - slot, WIN - 1)
        lives.append((last - back >= SINK) & (back != WIN - 1))
        raw = lax.dot_general(
            block(wide, j).astype(jnp.bfloat16), window_ref[i * BR + j, :, :half], NT,
            preferred_element_type=jnp.float32,
        )
        scores.append(jnp.where(lives[j], raw * HD ** (-0.5), NEG_BIG))
    s1 = jnp.concatenate(scores, axis=0)
    s2 = lax.dot_general(
        wide.astype(jnp.bfloat16), extra[:, :half], NT, preferred_element_type=jnp.float32
    ) * HD ** (-0.5)
    col = lax.broadcasted_iota(jnp.int32, s2.shape, 1)
    owner = lax.broadcasted_iota(jnp.int32, s2.shape, 0) // QH
    live2 = (jnp.where(col < BR * SINK, col // SINK, col - BR * SINK) == owner) & (t == 0)
    s2 = jnp.where(live2, s2, NEG_BIG)
    peak = jnp.maximum(jnp.max(s1, axis=1, keepdims=True), jnp.max(s2, axis=1, keepdims=True))
    w1 = jnp.exp(s1 - peak)
    w1 = jnp.concatenate([jnp.where(lives[j], block(w1, j), 0.0) for j in range(BR)], axis=0)
    w2 = jnp.where(live2, jnp.exp(s2 - peak), 0.0)
    total = jnp.sum(w1, axis=1, keepdims=True) + jnp.sum(w2, axis=1, keepdims=True)
    acc = jnp.concatenate(
        [
            jnp.dot(
                block(w1, j).astype(jnp.bfloat16), window_ref[i * BR + j, :, half:],
                preferred_element_type=jnp.float32,
            )
            for j in range(BR)
        ],
        axis=0,
    ) + jnp.dot(w2.astype(jnp.bfloat16), extra[:, half:], preferred_element_type=jnp.float32)
    heads_scr[...] = jnp.where(first_half, acc[:, :HD], acc[:, HD:])
    stat_scr[...] = jnp.where(lane == head_row, peak, 0.0) + jnp.where(
        lane == head_row + QH, total, 0.0
    )
    stats = functools.reduce(jnp.add, [stat_scr[pl.ds(h, BR, stride=QH), :] for h in range(QH)])
    per_chunk = summed_ref.shape[3] // HD
    for h in range(QH):
        summed_ref[h // per_chunk, i, :, (h % per_chunk) * HD : (h % per_chunk + 1) * HD] = heads_scr[
            pl.ds(h, BR, stride=QH), :
        ].astype(jnp.bfloat16)

    gate = projected_ref[0, i].astype(jnp.float32)
    x_pre = projected_ref[1, i]
    x = conv_rows([conv_state_ref[k, i] for k in range(3)], x_pre, taps_ref)
    step_x = step_ref[i] * x
    step_x_ref[i] = step_x
    decay = decay_ref[i]
    both = jnp.sum(in_f32 * out_rows.astype(jnp.float32), axis=1, keepdims=True)
    read_rows = []
    for j in range(BR):
        state = state_ref[i * BR + j]
        read_rows.append(
            lax.dot_general(out_rows, state, NT, preferred_element_type=jnp.float32)[j : j + 1, :]
        )
    readout = decay * jnp.concatenate(read_rows, axis=0) + step_x * both
    skip = jnp.concatenate(
        [by_head(skip_ref, g, (BR, 2 * MP)) for g in range(units // (2 * MP))], axis=1
    )
    gated = (readout + skip * x) * silu(gate)
    gated_ref[i] = gated
    square = jnp.sum(gated * gated, axis=1, keepdims=True)
    stats_ref[i] = jnp.where(
        lax.broadcasted_iota(jnp.int32, stats.shape, 1) == 2 * QH, square, stats
    )


def update_block(i, state_ref, coup_ref, step_x_ref, decay_ref, new_state_ref):
    in_f32 = coup_ref[i][:, :NS].astype(jnp.float32)
    step_x_t = step_x_ref[i].T
    decay_t = decay_ref[i].T
    for j in range(BR):
        new_state_ref[i * BR + j] = (
            decay_t[:, j : j + 1] * state_ref[i * BR + j].astype(jnp.float32)
            + step_x_t[:, j : j + 1] * in_f32[j : j + 1, :]
        ).astype(jnp.bfloat16)


def ahead(array):
    return pltpu.with_memory_space_constraint(array, pltpu.VMEM)


def keep(array):
    return pltpu.with_memory_space_constraint(array, pltpu.HBM)


def other(index, k, size):
    total, bit = 0, 1
    while bit < size:
        a, b = lax.rem(lax.div(index, bit), 2), lax.rem(lax.div(k, bit), 2)
        total = total + bit * (a + b - 2 * a * b)
        bit *= 2
    return total


def joint_kernel(
    tp_size, req_size, len_ref, skip_ref, qkv_ref, sink_ref, window_ref, state_ref, coup_ref,
    projected_ref, taps_ref, conv_state_ref, step_ref, decay_ref, mixer_gain_ref, residual_ref,
    final_gain_ref, mamba_out_ref, attention_out_ref, head_ref, new_residual_ref, new_state_ref,
    logits_ref, heads_scr, stat_scr, extra_scr, summed_ref, stats_ref, gated_ref, step_x_ref,
    mamba_buf, attention_buf, head_buf, sum_buf, stat_buf, part_out, part_buf, gather, final_buf,
    logit_out, sum_s, sum_r, stat_s, stat_r, part_s, part_r, gat_s, gat_r, log_s, log_r, load_sem,
):
    r = lax.axis_index("req")
    t = lax.axis_index("tp")
    rows = residual_ref.shape[0]
    blocks = rows // BR
    width = new_residual_ref.shape[1]
    peers = [other(t, q, tp_size) for q in range(tp_size)]
    reqs = [other(r, k, req_size) for k in range(req_size)]
    barrier = pltpu.get_barrier_semaphore()
    for q in range(1, tp_size):
        pl.semaphore_signal(barrier, inc=1, device_id=(r, peers[q]), device_id_type=MESH)
    for k in range(1, req_size):
        pl.semaphore_signal(barrier, inc=1, device_id=(reqs[k], t), device_id_type=MESH)
    load_mamba = pltpu.make_async_copy(mamba_out_ref, mamba_buf, load_sem.at[1])
    load_attention = pltpu.make_async_copy(attention_out_ref, attention_buf, load_sem.at[2])
    load_head = pltpu.make_async_copy(head_ref, head_buf, load_sem.at[3])
    for load in (load_mamba, load_attention, load_head):
        load.start()

    def mix(i, carry):
        mix_block(
            i, len_ref, skip_ref, qkv_ref, sink_ref, window_ref, state_ref, coup_ref, projected_ref,
            taps_ref, conv_state_ref, step_ref, decay_ref, summed_ref, stats_ref, gated_ref,
            step_x_ref, heads_scr, stat_scr, extra_scr,
        )
        return carry

    lax.fori_loop(0, blocks, mix, 0)
    pl.semaphore_wait(barrier, tp_size + req_size - 2)

    def send(src, dst, ssem, rsem, where):
        copy = pltpu.make_async_remote_copy(
            src_ref=src, dst_ref=dst, send_sem=ssem, recv_sem=rsem,
            device_id=where, device_id_type=MESH,
        )
        copy.start()
        return copy

    first = []
    for q in reversed(range(1, tp_size)):
        where = (r, peers[q])
        first.append(send(stats_ref, stat_buf.at[q], stat_s.at[q], stat_r.at[q], where))
        first.append(send(summed_ref.at[peers[q]], sum_buf.at[q], sum_s.at[q], sum_r.at[q], where))
    gated = gated_ref[...].reshape(rows, gated_ref.shape[2])
    mamba = (gated * mixer_gain_ref[...][None]).astype(jnp.bfloat16)
    columns = lambda p: pl.ds(pl.multiple_of(p * width, 128), width)
    load_mamba.wait()
    unscaled = [
        jnp.dot(mamba, mamba_buf[:, columns(peers[q])], preferred_element_type=jnp.float32)
        for q in range(tp_size)
    ]
    load_attention.wait()
    for copy in first:
        copy.wait()
    flat = lambda array: array.astype(jnp.float32).reshape(rows, array.shape[2])
    stats = [flat(stats_ref[...])] + [flat(stat_buf[q]) for q in range(1, tp_size)]
    sums = [flat(summed_ref[t])] + [flat(sum_buf[q]) for q in range(1, tp_size)]
    lane = lax.broadcasted_iota(jnp.int32, (rows, 128), 1)
    local_heads = QH // tp_size
    pieces = []
    for hl in range(local_heads):
        h = t * local_heads + hl
        peaks = [jnp.sum(jnp.where(lane == h, s, 0.0), axis=1, keepdims=True) for s in stats]
        totals = [jnp.sum(jnp.where(lane == h + QH, s, 0.0), axis=1, keepdims=True) for s in stats]
        top = functools.reduce(jnp.maximum, peaks)
        scales = [jnp.exp(p - top) for p in peaks]
        below = functools.reduce(jnp.add, [a * b for a, b in zip(scales, totals)])
        above = functools.reduce(
            jnp.add, [a * b[:, hl * HD : (hl + 1) * HD] for a, b in zip(scales, sums)]
        )
        pieces.append((above / below).astype(jnp.bfloat16))
    attended = jnp.concatenate(pieces, axis=1)
    square = functools.reduce(jnp.add, [s[:, 2 * QH : 2 * QH + 1] for s in stats])
    mamba_scale = lax.rsqrt(square / (MH * MP) + EPSILON)

    def partial(q):
        return mamba_scale * unscaled[q] + jnp.dot(
            attended, attention_buf[:, columns(peers[q])], preferred_element_type=jnp.float32
        )

    second = {}
    for q in reversed(range(1, tp_size)):
        part_out[q] = partial(q).astype(jnp.bfloat16)
        second[q] = send(part_out.at[q], part_buf.at[q], part_s.at[q], part_r.at[q], (r, peers[q]))
    mixed = residual_ref[:, columns(t)].astype(jnp.float32) + partial(0)
    for q in range(1, tp_size):
        second[q].wait()
        mixed = mixed + part_buf[q].astype(jnp.float32)
    fresh = mixed.astype(jnp.bfloat16)
    new_residual_ref[...] = fresh
    gather[0, 0] = fresh

    half = req_size // 2
    far_groups = list(range(half, req_size))
    near_groups = list(range(1, half))

    def move(k, src, dst, where):
        return pltpu.make_async_remote_copy(
            src_ref=gather.at[k if src else 0, src - 1 if src else 0], dst_ref=gather.at[k, dst],
            send_sem=gat_s.at[k, dst], recv_sem=gat_r.at[k, dst],
            device_id=where, device_id_type=MESH,
        )

    along = lambda k: move(k, 0, 0, (other(r, k, req_size), t))
    over = lambda k: move(k, 1, 2, (r, peers[2]))
    near = lambda k: move(k, 1, 1, (r, peers[1]))
    far = lambda k: move(k, 3, 3, (r, peers[1]))

    for k in far_groups + near_groups:
        along(k).start()
    for k in [0] + far_groups[:2] + near_groups + far_groups[2:]:
        if k:
            along(k).wait_recv()
        over(k).start()
        near(k).start()

    vocab = head_buf.shape[1]
    tile = min(512, vocab)
    each = rows // tp_size
    source = r * tp_size + t

    def pair_up(k):
        over(k).wait_recv()
        far(k).start()

    def logits_to(k, q):
        return pltpu.make_async_remote_copy(
            src_ref=logit_out.at[k, peers[q]], dst_ref=logits_ref.at[source],
            send_sem=log_s.at[k, q], recv_sem=log_r.at[k, q],
            device_id=(other(r, k, req_size), peers[q]), device_id_type=MESH,
        )

    own = pltpu.make_async_copy(logit_out.at[0, t], logits_ref.at[source], load_sem.at[0])
    pair_up(half)
    load_head.wait()

    def project(n, carry):
        k = lax.rem(n + half, req_size)
        near(k).wait_recv()
        far(k).wait_recv()
        values = [gather[k, i].astype(jnp.float32) for i in range(tp_size)]
        mean = functools.reduce(
            jnp.add, [jnp.sum(v * v, axis=1, keepdims=True) for v in values]
        ) / (width * tp_size)
        scale = lax.rsqrt(mean + EPSILON)
        for i in range(tp_size):
            cols = columns(peers[i])
            final_buf[:, cols] = (values[i] * scale * final_gain_ref[:, cols]).astype(jnp.bfloat16)

        @pl.when(n + 1 < req_size)
        def _():
            pair_up(lax.rem(n + 1 + half, req_size))

        def head_tile(c, carry):
            cols = pl.ds(pl.multiple_of(c * tile, 128), tile)
            part = jnp.dot(
                final_buf[...], head_buf[:, cols], preferred_element_type=jnp.float32
            )
            for q in range(tp_size):
                logit_out[k, q, :, cols] = part[q * each : (q + 1) * each, :].astype(jnp.bfloat16)
            return carry

        lax.fori_loop(0, vocab // tile, head_tile, 0)
        for q in reversed(range(1, tp_size)):
            logits_to(k, q).start()

        @pl.when(n != half)
        def _():
            logits_to(k, 0).start()

        return carry

    lax.fori_loop(0, req_size, project, 0)
    own.start()

    def update(i, carry):
        update_block(i, state_ref, coup_ref, step_x_ref, decay_ref, new_state_ref)
        return carry

    lax.fori_loop(0, blocks, update, 0)
    own.wait()

    def close(n, carry):
        k = lax.rem(n + half, req_size)
        for q in reversed(range(1, tp_size)):
            logits_to(k, q).wait()
        over(k).wait_send()
        near(k).wait_send()
        far(k).wait_send()

        @pl.when(n != half)
        def _():
            logits_to(k, 0).wait()
            along(k).wait_send()

        return carry

    lax.fori_loop(0, req_size, close, 0)


def joint(
    lengths, skip, qkv, sink, window, state, coup, projected, taps, conv_state, step, decay,
    mixer_gain, mamba_out, attention_out, residual, final_gain, output_head,
):
    tp_size = lax.axis_size("tp")
    req_size = lax.axis_size("req")
    rows, model = residual.shape
    units = step.shape[1]
    blocks = rows // BR
    width = model // tp_size
    chunk = QH * HD // tp_size
    each = rows // tp_size
    vocab = output_head.shape[1]

    def split(a):
        at = a.ndim - 2
        return a.reshape(a.shape[:at] + (blocks, BR) + a.shape[at + 1 :])

    dma = lambda *shape: pltpu.SemaphoreType.DMA(shape)
    vmem = pl.BlockSpec(memory_space=pltpu.VMEM)
    smem = pl.BlockSpec(memory_space=pltpu.SMEM)
    hbm = pl.BlockSpec(memory_space=pltpu.HBM)
    return pl.pallas_call(
        functools.partial(joint_kernel, tp_size, req_size),
        in_specs=[smem] * 2 + [vmem] * 13 + [hbm] * 3,
        out_specs=[vmem, vmem, hbm],
        out_shape=[
            jax.ShapeDtypeStruct((rows, width), jnp.bfloat16),
            jax.ShapeDtypeStruct(state.shape, jnp.bfloat16),
            jax.ShapeDtypeStruct((req_size * tp_size, each, vocab), jnp.bfloat16),
        ],
        scratch_shapes=[
            pltpu.VMEM((BR * QH, HD), jnp.float32),
            pltpu.VMEM((BR * QH, HD), jnp.float32),
            pltpu.VMEM((BR * QH, 2 * KVH * HD), jnp.float32),
            pltpu.VMEM((tp_size, blocks, BR, chunk), jnp.bfloat16),
            pltpu.VMEM((blocks, BR, 128), jnp.float32),
            pltpu.VMEM((blocks, BR, units), jnp.float32),
            pltpu.VMEM((blocks, BR, units), jnp.float32),
            pltpu.VMEM(mamba_out.shape, jnp.bfloat16),
            pltpu.VMEM(attention_out.shape, jnp.bfloat16),
            pltpu.VMEM(output_head.shape, jnp.bfloat16),
            pltpu.VMEM((tp_size, blocks, BR, chunk), jnp.bfloat16),
            pltpu.VMEM((tp_size, blocks, BR, 128), jnp.float32),
            pltpu.VMEM((tp_size, rows, width), jnp.bfloat16),
            pltpu.VMEM((tp_size, rows, width), jnp.bfloat16),
            pltpu.VMEM((req_size, tp_size, rows, width), jnp.bfloat16),
            pltpu.VMEM((rows, model), jnp.bfloat16),
            pltpu.VMEM((req_size, tp_size, each, vocab), jnp.bfloat16),
            dma(tp_size), dma(tp_size), dma(tp_size), dma(tp_size), dma(tp_size), dma(tp_size),
            dma(req_size, tp_size), dma(req_size, tp_size), dma(req_size, tp_size),
            dma(req_size, tp_size), dma(4),
        ],
        cost_estimate=pl.CostEstimate(
            flops=40_000_000_000, bytes_accessed=30_000_000, transcendentals=0
        ),
        compiler_params=pltpu.CompilerParams(
            collective_id=1, has_side_effects=True, vmem_limit_bytes=24 << 20
        ),
    )(
        lengths, skip, split(qkv), sink, ahead(window), ahead(state), split(coup), split(projected),
        taps, split(conv_state), split(step), split(decay), mixer_gain, residual, final_gain[None],
        keep(mamba_out), keep(attention_out), keep(output_head),
    )


def finish_kernel(
    residual_ref, blocks_ref, state_ref, conv_ref, projected_ref, coup_ref, pre_ref, qkv_ref,
    new_residual_ref, logits_ref, new_state_ref, new_conv_ref, new_coup_ref, key_value_ref, sem,
):
    copy = pltpu.make_async_copy(state_ref, new_state_ref, sem.at[0])
    step = pl.program_id(0)

    @pl.when(step == 0)
    def _():
        copy.start()
        new_residual_ref[...] = residual_ref[...]
        new_conv_ref[0] = conv_ref[1]
        new_conv_ref[1] = conv_ref[2]
        new_conv_ref[2] = projected_ref[1]
        new_coup_ref[0] = coup_ref[1]
        new_coup_ref[1] = coup_ref[2]
        new_coup_ref[2] = pre_ref[...]
        key_value_ref[...] = qkv_ref[:, QH * HD :]

    width = blocks_ref.shape[2]
    for n in range(blocks_ref.shape[0]):
        logits_ref[:, n * width : (n + 1) * width] = blocks_ref[n].astype(jnp.float32)

    @pl.when(step == pl.num_programs(0) - 1)
    def _():
        copy.wait()


def finish(residual, blocks, state, conv_state, projected, coup_state, pre, qkv):
    count, each, vocab = blocks.shape
    steps = 4
    part = count // steps
    shaped = lambda a: jax.ShapeDtypeStruct(a.shape, a.dtype)
    whole = lambda shape: pl.BlockSpec(shape, lambda i: (0,) * len(shape))
    key_value = (qkv.shape[0], qkv.shape[1] - QH * HD)
    return pl.pallas_call(
        finish_kernel,
        grid=(steps,),
        in_specs=[
            whole(residual.shape),
            pl.BlockSpec((part, each, vocab), lambda i: (i, 0, 0)),
            pl.BlockSpec(memory_space=pl.ANY),
            whole(conv_state.shape), whole(projected.shape), whole(coup_state.shape),
            whole(pre.shape), whole(qkv.shape),
        ],
        out_specs=[
            whole(residual.shape),
            pl.BlockSpec((each, part * vocab), lambda i: (0, i)),
            pl.BlockSpec(memory_space=pltpu.HBM),
            whole(conv_state.shape), whole(coup_state.shape), whole(key_value),
        ],
        out_shape=[
            shaped(residual),
            jax.ShapeDtypeStruct((each, count * vocab), jnp.float32),
            shaped(state), shaped(conv_state), shaped(coup_state),
            jax.ShapeDtypeStruct(key_value, qkv.dtype),
        ],
        scratch_shapes=[pltpu.SemaphoreType.DMA((1,))],
        compiler_params=pltpu.CompilerParams(vmem_limit_bytes=8 << 20),
    )(residual, blocks, state, conv_state, projected, coup_state, pre, qkv)


def body(
    residual,
    cache_lengths,
    input_gain,
    inner_weight,
    step_weight,
    step_bias,
    decay_log,
    skip_gain,
    conv_weight,
    conv_state,
    coupling_weight,
    coupling_conv,
    coupling_state,
    scan_state,
    mixer_gain,
    attention_weight,
    sink_cache,
    window_cache,
    mamba_out,
    attention_out,
    final_gain,
    output_head,
):
    row_count = residual.shape[0]
    local_units = inner_weight.shape[2]
    swap = lambda array: jnp.transpose(array, (1, 0, 2))
    coup_state = swap(coupling_state)
    normed, coupling_pre, qkv_rows, coupling_all, step_size, decay_rate = entry(
        step_bias, decay_log, residual, input_gain, attention_weight, coupling_weight,
        coupling_conv, coup_state, step_weight.T,
    )
    projected = jnp.einsum(
        "rd,dtc->trc", normed, inner_weight, preferred_element_type=jnp.float32
    ).astype(jnp.bfloat16)
    conv_rows_first = swap(conv_state)
    fresh_residual, fresh_state, blocks = joint(
        cache_lengths, skip_gain, qkv_rows, sink_cache, window_cache,
        scan_state.reshape(row_count, local_units, NS), coupling_all, projected, conv_weight,
        conv_rows_first, step_size, decay_rate, mixer_gain, mamba_out, attention_out, residual,
        final_gain, output_head,
    )
    new_residual, logits, new_state, new_conv, new_coup, new_key_value = finish(
        fresh_residual, blocks, fresh_state, conv_rows_first, projected, coup_state, coupling_pre,
        qkv_rows,
    )
    new_conv_state = swap(new_conv)
    new_coupling_state = swap(new_coup)
    new_scan_state = new_state.reshape(scan_state.shape)
    return (new_residual, logits, new_scan_state, new_conv_state, new_coupling_state, new_key_value)


def solution(mesh):
    return jax.shard_map(
        body,
        mesh=mesh,
        in_specs=(
            P("req", None),
            P("req"),
            P(),
            P(None, None, "tp"),
            P(None, "tp"),
            P("tp"),
            P("tp"),
            P("tp"),
            P(None, "tp"),
            P("req", None, "tp"),
            P(None, "tp"),
            P(None, "tp"),
            P("req", None, "tp"),
            P("req", "tp", None, None),
            P("tp"),
            P(None, "tp"),
            P("req", None, None),
            P("req", "tp", None),
            P("tp", None),
            P("tp", None),
            P(),
            P(None, ("req", "tp")),
        ),
        out_specs=(
            P("req", "tp"),
            P(("req", "tp"), None),
            P("req", "tp", None, None),
            P("req", None, "tp"),
            P("req", None, "tp"),
            P("req", None),
        ),
        check_vma=False,
    )
```

```python
import functools

import jax
import jax.numpy as jnp
from jax import lax
from jax.experimental import pallas as pl
from jax.experimental.pallas import tpu as pltpu
from jax.sharding import PartitionSpec as P

MH = 24
MP = 64
NS = 256
QH = 8
KVH = 2
HD = 128
WIN = 1024
SINK = 4
BR = 8

EPSILON = 1e-05
NEG_BIG = -1e30
MESH = pl.DeviceIdType.MESH
NT = (((1,), (1,)), ((), ()))


def norm_rows(values, gain):
    widened = values.astype(jnp.float32)
    mean_sq = jnp.mean(widened * widened, axis=-1, keepdims=True)
    return (widened * lax.rsqrt(mean_sq + EPSILON) * gain).astype(jnp.bfloat16)


def silu(v):
    return v / (1.0 + jnp.exp(-v))


def conv_rows(old, fresh, taps_ref):
    steps = [row.astype(jnp.float32) for row in (*old, fresh)]
    taps = taps_ref[...].astype(jnp.float32)
    mixed = steps[0] * taps[0:1]
    for k in range(1, 4):
        mixed = mixed + steps[k] * taps[k : k + 1]
    return silu(mixed)


def by_head(ref, g, shape):
    lane = lax.broadcasted_iota(jnp.int32, shape, 1)
    return jnp.where(lane < MP, ref[2 * g], ref[2 * g + 1])


def entry_kernel(
    tp_size, bias_src, log_src, residual_src, gain_src, attention_src, coupling_src, taps_src,
    state_src, step_weight_src, normed_ref, pre_ref, qkv_ref, coup_ref, step_ref, decay_ref,
    residual_ref, gain_ref, attention_ref, coupling_ref, taps_ref,
    state_ref, step_weight_ref, bias_ref, log_ref, load_sem, qkv_s, qkv_r, coup_s, coup_r,
):
    r = lax.axis_index("req")
    t = lax.axis_index("tp")
    peers = [lax.rem(t + k, tp_size) for k in range(tp_size)]
    barrier = pltpu.get_barrier_semaphore()
    for k in range(1, tp_size):
        pl.semaphore_signal(barrier, inc=1, device_id=(r, peers[k]), device_id_type=MESH)
    sources = [
        residual_src, gain_src, attention_src, coupling_src, taps_src, state_src, step_weight_src,
        bias_src, log_src,
    ]
    places = [
        residual_ref, gain_ref, attention_ref, coupling_ref, taps_ref, state_ref, step_weight_ref,
        bias_ref, log_ref,
    ]
    loads = [
        pltpu.make_async_copy(src, dst, load_sem.at[n])
        for n, (src, dst) in enumerate(zip(sources, places))
    ]
    for load in loads:
        load.start()
    loads[0].wait()
    loads[1].wait()
    normed = norm_rows(residual_ref[...], gain_ref[...])
    normed_ref[...] = normed
    copies = []

    def share(out_ref, value, ssem, rsem):
        width = value.shape[1]
        cols = pl.ds(pl.multiple_of(t * width, 128), width)
        out_ref[:, cols] = value
        for k in range(1, tp_size):
            copy = pltpu.make_async_remote_copy(
                src_ref=out_ref.at[:, cols], dst_ref=out_ref.at[:, cols], send_sem=ssem.at[k],
                recv_sem=rsem.at[k], device_id=(r, peers[k]), device_id_type=MESH,
            )
            copy.start()
            copies.append(copy)

    loads[2].wait()
    qkv = jnp.dot(normed, attention_ref[...], preferred_element_type=jnp.float32)
    pl.semaphore_wait(barrier, tp_size - 1)
    share(qkv_ref, qkv.astype(jnp.bfloat16), qkv_s, qkv_r)
    for load in loads[3:]:
        load.wait()
    pre = jnp.dot(normed, coupling_ref[...], preferred_element_type=jnp.float32).astype(jnp.bfloat16)
    pre_ref[...] = pre
    share(coup_ref, conv_rows([state_ref[k] for k in range(3)], pre, taps_ref).astype(jnp.bfloat16), coup_s, coup_r)
    steps = (
        lax.dot_general(normed, step_weight_ref[...], NT, preferred_element_type=jnp.float32)
        .astype(jnp.bfloat16)
        .astype(jnp.float32)
    )
    shape = (normed.shape[0], 2 * MP)
    for g in range(steps.shape[1] // 2):
        lane = lax.broadcasted_iota(jnp.int32, shape, 1)
        v = jnp.where(lane < MP, steps[:, 2 * g : 2 * g + 1], steps[:, 2 * g + 1 : 2 * g + 2])
        v = v + by_head(bias_ref, g, shape)
        size = jnp.maximum(v, 0.0) + jnp.log1p(jnp.exp(-jnp.abs(v)))
        step_ref[:, g * 2 * MP : (g + 1) * 2 * MP] = size
        decay_ref[:, g * 2 * MP : (g + 1) * 2 * MP] = jnp.exp(
            -size * jnp.exp(by_head(log_ref, g, shape))
        )
    for copy in copies:
        copy.wait()


def entry(bias, decay_log, residual, gain, attention_weight, coupling_weight, taps, state, step_weight):
    tp_size = lax.axis_size("tp")
    rows, model = residual.shape
    units = bias.shape[0] * MP
    vmem = pl.BlockSpec(memory_space=pltpu.VMEM)
    hbm = pl.BlockSpec(memory_space=pltpu.HBM)
    dma = pltpu.SemaphoreType.DMA((tp_size,))
    operands = (residual, gain[None], attention_weight, coupling_weight, taps, state, step_weight)
    levels = (bias, decay_log)
    shaped = jax.ShapeDtypeStruct
    return pl.pallas_call(
        functools.partial(entry_kernel, tp_size),
        in_specs=[hbm] * 9,
        out_specs=[vmem] * 6,
        out_shape=[
            shaped((rows, model), jnp.bfloat16),
            shaped((rows, coupling_weight.shape[1]), jnp.bfloat16),
            shaped((rows, attention_weight.shape[1] * tp_size), jnp.bfloat16),
            shaped((rows, coupling_weight.shape[1] * tp_size), jnp.bfloat16),
            shaped((rows, units), jnp.float32),
            shaped((rows, units), jnp.float32),
        ],
        scratch_shapes=[pltpu.VMEM(a.shape, a.dtype) for a in operands]
        + [pltpu.SMEM(a.shape, a.dtype) for a in levels]
        + [pltpu.SemaphoreType.DMA((len(operands) + len(levels),))]
        + [dma] * 4,
        cost_estimate=pl.CostEstimate(flops=9_000_000_000, bytes_accessed=3_000_000, transcendentals=0),
        compiler_params=pltpu.CompilerParams(
            collective_id=0, has_side_effects=True, vmem_limit_bytes=8 << 20
        ),
    )(*map(keep, levels), *map(keep, operands))


def attend_block(
    i, len_ref, qkv_ref, sink_ref, window_ref, summed_ref, stats_ref, heads_scr, stat_scr, extra_scr
):
    half = KVH * HD
    group = QH // KVH
    t = lax.axis_index("tp")
    slots = window_ref.shape[1]
    qkv = qkv_ref[i]
    fresh = qkv[:, QH * HD :]

    for h in range(QH):
        heads_scr[pl.ds(h, BR, stride=QH), :] = qkv[:, h * HD : (h + 1) * HD].astype(jnp.float32)
    for j in range(BR):
        extra_scr[j * SINK : (j + 1) * SINK, :] = sink_ref[i * BR + j].astype(jnp.float32)
    extra_scr[BR * SINK : BR * SINK + BR, :] = fresh.astype(jnp.float32)
    extra_scr[BR * SINK + BR :, :] = jnp.zeros_like(extra_scr[BR * SINK + BR :, :])
    extra = extra_scr[...].astype(jnp.bfloat16)
    head_row = lax.broadcasted_iota(jnp.int32, (BR * QH, HD), 0) % QH
    lane = lax.broadcasted_iota(jnp.int32, (BR * QH, HD), 1)
    first_half = head_row < group
    q = heads_scr[...]
    wide = jnp.concatenate([jnp.where(first_half, q, 0.0), jnp.where(first_half, 0.0, q)], axis=1)
    block = lambda array, j: array[j * QH : (j + 1) * QH]
    slot = t * slots + lax.broadcasted_iota(jnp.int32, (QH, slots), 1)
    lives, scores = [], []
    for j in range(BR):
        last = len_ref[i * BR + j] - 1
        back = jnp.bitwise_and(last - slot, WIN - 1)
        lives.append((last - back >= SINK) & (back != WIN - 1))
        raw = lax.dot_general(
            block(wide, j).astype(jnp.bfloat16), window_ref[i * BR + j, :, :half], NT,
            preferred_element_type=jnp.float32,
        )
        scores.append(jnp.where(lives[j], raw * HD ** (-0.5), NEG_BIG))
    s1 = jnp.concatenate(scores, axis=0)
    s2 = lax.dot_general(
        wide.astype(jnp.bfloat16), extra[:, :half], NT, preferred_element_type=jnp.float32
    ) * HD ** (-0.5)
    col = lax.broadcasted_iota(jnp.int32, s2.shape, 1)
    owner = lax.broadcasted_iota(jnp.int32, s2.shape, 0) // QH
    live2 = (jnp.where(col < BR * SINK, col // SINK, col - BR * SINK) == owner) & (t == 0)
    s2 = jnp.where(live2, s2, NEG_BIG)
    peak = jnp.maximum(jnp.max(s1, axis=1, keepdims=True), jnp.max(s2, axis=1, keepdims=True))
    w1 = jnp.exp(s1 - peak)
    w1 = jnp.concatenate([jnp.where(lives[j], block(w1, j), 0.0) for j in range(BR)], axis=0)
    w2 = jnp.where(live2, jnp.exp(s2 - peak), 0.0)
    total = jnp.sum(w1, axis=1, keepdims=True) + jnp.sum(w2, axis=1, keepdims=True)
    acc = jnp.concatenate(
        [
            jnp.dot(
                block(w1, j).astype(jnp.bfloat16), window_ref[i * BR + j, :, half:],
                preferred_element_type=jnp.float32,
            )
            for j in range(BR)
        ],
        axis=0,
    ) + jnp.dot(w2.astype(jnp.bfloat16), extra[:, half:], preferred_element_type=jnp.float32)
    heads_scr[...] = jnp.where(first_half, acc[:, :HD], acc[:, HD:])
    stat_scr[...] = jnp.where(lane == head_row, peak, 0.0) + jnp.where(
        lane == head_row + QH, total, 0.0
    )
    stats_ref[i] = functools.reduce(
        jnp.add, [stat_scr[pl.ds(h, BR, stride=QH), :] for h in range(QH)]
    )
    per_chunk = summed_ref.shape[3] // HD
    for h in range(QH):
        summed_ref[h // per_chunk, i, :, (h % per_chunk) * HD : (h % per_chunk + 1) * HD] = heads_scr[
            pl.ds(h, BR, stride=QH), :
        ].astype(jnp.bfloat16)


def scan_block(
    i, skip_ref, state_ref, coup_ref, projected_ref, taps_ref, conv_state_ref, step_ref, decay_ref,
    gated_ref, square_ref, step_x_ref,
):
    units = step_ref.shape[2]
    coup = coup_ref[i]
    out_rows = coup[:, NS:]
    in_f32 = coup[:, :NS].astype(jnp.float32)
    gate = projected_ref[0, i].astype(jnp.float32)
    x_pre = projected_ref[1, i]
    x = conv_rows([conv_state_ref[k, i] for k in range(3)], x_pre, taps_ref)
    step_x = step_ref[i] * x
    step_x_ref[i] = step_x
    decay = decay_ref[i]
    both = jnp.sum(in_f32 * out_rows.astype(jnp.float32), axis=1, keepdims=True)
    read_rows = []
    for j in range(BR):
        state = state_ref[i * BR + j]
        read_rows.append(
            lax.dot_general(out_rows, state, NT, preferred_element_type=jnp.float32)[j : j + 1, :]
        )
    readout = decay * jnp.concatenate(read_rows, axis=0) + step_x * both
    skip = jnp.concatenate(
        [by_head(skip_ref, g, (BR, 2 * MP)) for g in range(units // (2 * MP))], axis=1
    )
    gated = (readout + skip * x) * silu(gate)
    gated_ref[i] = gated
    square_ref[i] = jnp.broadcast_to(
        jnp.sum(gated * gated, axis=1, keepdims=True), square_ref.shape[1:]
    )


def update_block(i, state_ref, coup_ref, step_x_ref, decay_ref, new_state_ref):
    in_f32 = coup_ref[i][:, :NS].astype(jnp.float32)
    step_x_t = step_x_ref[i].T
    decay_t = decay_ref[i].T
    for j in range(BR):
        new_state_ref[i * BR + j] = (
            decay_t[:, j : j + 1] * state_ref[i * BR + j].astype(jnp.float32)
            + step_x_t[:, j : j + 1] * in_f32[j : j + 1, :]
        ).astype(jnp.bfloat16)


def ahead(array):
    return pltpu.with_memory_space_constraint(array, pltpu.VMEM)


def keep(array):
    return pltpu.with_memory_space_constraint(array, pltpu.HBM)


def other(index, k, size):
    total, bit = 0, 1
    while bit < size:
        a, b = lax.rem(lax.div(index, bit), 2), lax.rem(lax.div(k, bit), 2)
        total = total + bit * (a + b - 2 * a * b)
        bit *= 2
    return total


def joint_kernel(
    tp_size, req_size, len_ref, skip_ref, qkv_ref, sink_ref, window_ref, state_ref, coup_ref,
    projected_ref, taps_ref, conv_state_ref, step_ref, decay_ref, mixer_gain_ref, residual_ref,
    final_gain_ref, mamba_out_ref, attention_out_ref, head_ref, new_residual_ref, new_state_ref,
    logits_ref, heads_scr, stat_scr, extra_scr, summed_ref, stats_ref, gated_ref, square_ref,
    step_x_ref, square_buf, scan_out, scan_buf, mamba_buf, attention_buf, head_buf, sum_buf, stat_buf, part_out, part_buf, gather, final_buf,
    logit_out, square_s, square_r, scan_s, scan_r, sum_s, sum_r, stat_s, stat_r, part_s, part_r, gat_s, gat_r, log_s, log_r, load_sem,
):
    r = lax.axis_index("req")
    t = lax.axis_index("tp")
    rows = residual_ref.shape[0]
    blocks = rows // BR
    width = new_residual_ref.shape[1]
    peers = [other(t, q, tp_size) for q in range(tp_size)]
    reqs = [other(r, k, req_size) for k in range(req_size)]
    barrier = pltpu.get_barrier_semaphore()
    for q in range(1, tp_size):
        pl.semaphore_signal(barrier, inc=1, device_id=(r, peers[q]), device_id_type=MESH)
    for k in range(1, req_size):
        pl.semaphore_signal(barrier, inc=1, device_id=(reqs[k], t), device_id_type=MESH)
    load_mamba = pltpu.make_async_copy(mamba_out_ref, mamba_buf, load_sem.at[1])
    load_attention = pltpu.make_async_copy(attention_out_ref, attention_buf, load_sem.at[2])
    load_head = pltpu.make_async_copy(head_ref, head_buf, load_sem.at[3])
    for load in (load_mamba, load_attention, load_head):
        load.start()

    def attend(i, carry):
        attend_block(
            i, len_ref, qkv_ref, sink_ref, window_ref, summed_ref, stats_ref, heads_scr, stat_scr,
            extra_scr,
        )
        return carry

    lax.fori_loop(0, blocks, attend, 0)
    pl.semaphore_wait(barrier, tp_size + req_size - 2)

    def send(src, dst, ssem, rsem, where):
        copy = pltpu.make_async_remote_copy(
            src_ref=src, dst_ref=dst, send_sem=ssem, recv_sem=rsem,
            device_id=where, device_id_type=MESH,
        )
        copy.start()
        return copy

    first = []
    for q in reversed(range(1, tp_size)):
        where = (r, peers[q])
        first.append(send(stats_ref, stat_buf.at[q], stat_s.at[q], stat_r.at[q], where))
        first.append(send(summed_ref.at[peers[q]], sum_buf.at[q], sum_s.at[q], sum_r.at[q], where))

    def scan(i, carry):
        scan_block(
            i, skip_ref, state_ref, coup_ref, projected_ref, taps_ref, conv_state_ref, step_ref,
            decay_ref, gated_ref, square_ref, step_x_ref,
        )
        return carry

    lax.fori_loop(0, blocks, scan, 0)
    gated = gated_ref[...].reshape(rows, gated_ref.shape[2])
    mamba = (gated * mixer_gain_ref[...][None]).astype(jnp.bfloat16)
    columns = lambda p: pl.ds(pl.multiple_of(p * width, 128), width)
    load_mamba.wait()

    def unscaled(q):
        return jnp.dot(mamba, mamba_buf[:, columns(peers[q])], preferred_element_type=jnp.float32)

    between = []
    for q in reversed(range(1, tp_size)):
        where = (r, peers[q])
        between.append(send(square_ref, square_buf.at[q], square_s.at[q], square_r.at[q], where))
        scan_out[q] = unscaled(q).astype(jnp.bfloat16)
        between.append(send(scan_out.at[q], scan_buf.at[q], scan_s.at[q], scan_r.at[q], where))
    scanned = unscaled(0)
    load_attention.wait()
    for copy in first:
        copy.wait()
    flat = lambda array: array.astype(jnp.float32).reshape(rows, array.shape[2])
    stats = [flat(stats_ref[...])] + [flat(stat_buf[q]) for q in range(1, tp_size)]
    sums = [flat(summed_ref[t])] + [flat(sum_buf[q]) for q in range(1, tp_size)]
    lane = lax.broadcasted_iota(jnp.int32, (rows, 128), 1)
    local_heads = QH // tp_size
    pieces = []
    for hl in range(local_heads):
        h = t * local_heads + hl
        peaks = [jnp.sum(jnp.where(lane == h, s, 0.0), axis=1, keepdims=True) for s in stats]
        totals = [jnp.sum(jnp.where(lane == h + QH, s, 0.0), axis=1, keepdims=True) for s in stats]
        top = functools.reduce(jnp.maximum, peaks)
        scales = [jnp.exp(p - top) for p in peaks]
        below = functools.reduce(jnp.add, [a * b for a, b in zip(scales, totals)])
        above = functools.reduce(
            jnp.add, [a * b[:, hl * HD : (hl + 1) * HD] for a, b in zip(scales, sums)]
        )
        pieces.append((above / below).astype(jnp.bfloat16))
    attended = jnp.concatenate(pieces, axis=1)

    def partial(q):
        return jnp.dot(
            attended, attention_buf[:, columns(peers[q])], preferred_element_type=jnp.float32
        )

    second = {}
    for q in reversed(range(1, tp_size)):
        part_out[q] = partial(q).astype(jnp.bfloat16)
        second[q] = send(part_out.at[q], part_buf.at[q], part_s.at[q], part_r.at[q], (r, peers[q]))
    mixed = residual_ref[:, columns(t)].astype(jnp.float32) + partial(0)
    for copy in between:
        copy.wait()
    square = flat(square_ref[...])[:, :1]
    for q in range(1, tp_size):
        square = square + flat(square_buf[q])[:, :1]
        scanned = scanned + scan_buf[q].astype(jnp.float32)
    mixed = mixed + scanned * lax.rsqrt(square / (MH * MP) + EPSILON)
    for q in range(1, tp_size):
        second[q].wait()
        mixed = mixed + part_buf[q].astype(jnp.float32)
    fresh = mixed.astype(jnp.bfloat16)
    new_residual_ref[...] = fresh
    gather[0, 0] = fresh

    half = req_size // 2
    far_groups = list(range(half, req_size))
    near_groups = list(range(1, half))

    def move(k, src, dst, where):
        return pltpu.make_async_remote_copy(
            src_ref=gather.at[k if src else 0, src - 1 if src else 0], dst_ref=gather.at[k, dst],
            send_sem=gat_s.at[k, dst], recv_sem=gat_r.at[k, dst],
            device_id=where, device_id_type=MESH,
        )

    along = lambda k: move(k, 0, 0, (other(r, k, req_size), t))
    over = lambda k: move(k, 1, 2, (r, peers[2]))
    near = lambda k: move(k, 1, 1, (r, peers[1]))
    far = lambda k: move(k, 3, 3, (r, peers[1]))

    def spread(k):
        if k:
            along(k).wait_recv()
        over(k).start()
        near(k).start()

    def pair_up(k):
        over(k).wait_recv()
        far(k).start()

    along(half).start()
    for k in far_groups[1:] + near_groups:
        along(k).start()
    spread(half)
    spread(0)
    spread(half + 1)
    for k in near_groups:
        spread(k)
    pair_up(half)
    for k in far_groups[2:3]:
        spread(k)

    vocab = head_buf.shape[1]
    tile = min(512, vocab)
    each = rows // tp_size
    source = r * tp_size + t

    def logits_to(k, q):
        return pltpu.make_async_remote_copy(
            src_ref=logit_out.at[k, peers[q]], dst_ref=logits_ref.at[source],
            send_sem=log_s.at[k, q], recv_sem=log_r.at[k, q],
            device_id=(other(r, k, req_size), peers[q]), device_id_type=MESH,
        )

    own = pltpu.make_async_copy(logit_out.at[0, t], logits_ref.at[source], load_sem.at[0])
    def group_at(n):
        late = lax.div(n, half)
        return (1 - late) * (n + half) + late * (req_size - 1 - n)

    load_head.wait()

    def project(n, carry):
        k = group_at(n)
        near(k).wait_recv()
        far(k).wait_recv()
        squares = jnp.zeros((rows, width), jnp.float32)
        for i in range(tp_size):
            value = gather[k, i].astype(jnp.float32)
            squares = squares + value * value
        mean = jnp.sum(squares, axis=1, keepdims=True) / (width * tp_size)
        scale = lax.rsqrt(mean + EPSILON)
        for i in range(tp_size):
            cols = columns(peers[i])
            final_buf[:, cols] = (
                gather[k, i].astype(jnp.float32) * scale * final_gain_ref[:, cols]
            ).astype(jnp.bfloat16)

        @pl.when(n + 1 < req_size)
        def _():
            pair_up(group_at(n + 1))

        def head_tile(c, carry):
            cols = pl.ds(pl.multiple_of(c * tile, 128), tile)
            part = jnp.dot(
                final_buf[...], head_buf[:, cols], preferred_element_type=jnp.float32
            )
            for q in range(tp_size):
                logit_out[k, q, :, cols] = part[q * each : (q + 1) * each, :].astype(jnp.bfloat16)
            return carry

        lax.fori_loop(0, vocab // tile, head_tile, 0)
        for q in reversed(range(1, tp_size)):
            logits_to(k, q).start()

        @pl.when(n != req_size - 1)
        def _():
            logits_to(k, 0).start()

        @pl.when(n == 0)
        def _():
            for later in far_groups[3:]:
                spread(later)

        @pl.when(n == req_size - 1)
        def _():
            own.start()

        return carry

    lax.fori_loop(0, req_size, project, 0)
    def update(i, carry):
        update_block(i, state_ref, coup_ref, step_x_ref, decay_ref, new_state_ref)
        return carry

    lax.fori_loop(0, blocks, update, 0)
    own.wait()

    def close(n, carry):
        k = group_at(n)
        for q in reversed(range(1, tp_size)):
            logits_to(k, q).wait()
        over(k).wait_send()
        near(k).wait_send()
        far(k).wait_send()

        @pl.when(n != req_size - 1)
        def _():
            logits_to(k, 0).wait()
            along(k).wait_send()

        return carry

    lax.fori_loop(0, req_size, close, 0)


def joint(
    lengths, skip, qkv, sink, window, state, coup, projected, taps, conv_state, step, decay,
    mixer_gain, mamba_out, attention_out, residual, final_gain, output_head,
):
    tp_size = lax.axis_size("tp")
    req_size = lax.axis_size("req")
    rows, model = residual.shape
    units = step.shape[1]
    blocks = rows // BR
    width = model // tp_size
    chunk = QH * HD // tp_size
    each = rows // tp_size
    vocab = output_head.shape[1]

    def split(a):
        at = a.ndim - 2
        return a.reshape(a.shape[:at] + (blocks, BR) + a.shape[at + 1 :])

    dma = lambda *shape: pltpu.SemaphoreType.DMA(shape)
    vmem = pl.BlockSpec(memory_space=pltpu.VMEM)
    smem = pl.BlockSpec(memory_space=pltpu.SMEM)
    hbm = pl.BlockSpec(memory_space=pltpu.HBM)
    return pl.pallas_call(
        functools.partial(joint_kernel, tp_size, req_size),
        in_specs=[smem] * 2 + [vmem] * 13 + [hbm] * 3,
        out_specs=[vmem, vmem, hbm],
        out_shape=[
            jax.ShapeDtypeStruct((rows, width), jnp.bfloat16),
            jax.ShapeDtypeStruct(state.shape, jnp.bfloat16),
            jax.ShapeDtypeStruct((req_size * tp_size, each, vocab), jnp.bfloat16),
        ],
        scratch_shapes=[
            pltpu.VMEM((BR * QH, HD), jnp.float32),
            pltpu.VMEM((BR * QH, HD), jnp.float32),
            pltpu.VMEM((BR * QH, 2 * KVH * HD), jnp.float32),
            pltpu.VMEM((tp_size, blocks, BR, chunk), jnp.bfloat16),
            pltpu.VMEM((blocks, BR, 128), jnp.float32),
            pltpu.VMEM((blocks, BR, units), jnp.float32),
            pltpu.VMEM((blocks, BR, 128), jnp.float32),
            pltpu.VMEM((blocks, BR, units), jnp.float32),
            pltpu.VMEM((tp_size, blocks, BR, 128), jnp.float32),
            pltpu.VMEM((tp_size, rows, width), jnp.bfloat16),
            pltpu.VMEM((tp_size, rows, width), jnp.bfloat16),
            pltpu.VMEM(mamba_out.shape, jnp.bfloat16),
            pltpu.VMEM(attention_out.shape, jnp.bfloat16),
            pltpu.VMEM(output_head.shape, jnp.bfloat16),
            pltpu.VMEM((tp_size, blocks, BR, chunk), jnp.bfloat16),
            pltpu.VMEM((tp_size, blocks, BR, 128), jnp.float32),
            pltpu.VMEM((tp_size, rows, width), jnp.bfloat16),
            pltpu.VMEM((tp_size, rows, width), jnp.bfloat16),
            pltpu.VMEM((req_size, tp_size, rows, width), jnp.bfloat16),
            pltpu.VMEM((rows, model), jnp.bfloat16),
            pltpu.VMEM((req_size, tp_size, each, vocab), jnp.bfloat16),
            dma(tp_size), dma(tp_size), dma(tp_size), dma(tp_size), dma(tp_size), dma(tp_size),
            dma(tp_size), dma(tp_size), dma(tp_size), dma(tp_size),
            dma(req_size, tp_size), dma(req_size, tp_size), dma(req_size, tp_size),
            dma(req_size, tp_size), dma(4),
        ],
        cost_estimate=pl.CostEstimate(
            flops=40_000_000_000, bytes_accessed=30_000_000, transcendentals=0
        ),
        compiler_params=pltpu.CompilerParams(
            collective_id=1, has_side_effects=True, vmem_limit_bytes=24 << 20
        ),
    )(
        lengths, skip, split(qkv), sink, ahead(window), ahead(state), split(coup), split(projected),
        taps, split(conv_state), split(step), split(decay), mixer_gain, residual, final_gain[None],
        keep(mamba_out), keep(attention_out), keep(output_head),
    )


def finish_kernel(
    residual_ref, blocks_ref, state_ref, conv_ref, projected_ref, coup_ref, pre_ref, qkv_ref,
    new_residual_ref, logits_ref, new_state_ref, new_conv_ref, new_coup_ref, key_value_ref, sem,
):
    copy = pltpu.make_async_copy(state_ref, new_state_ref, sem.at[0])
    step = pl.program_id(0)

    @pl.when(step == 0)
    def _():
        copy.start()
        new_residual_ref[...] = residual_ref[...]
        new_conv_ref[0] = conv_ref[1]
        new_conv_ref[1] = conv_ref[2]
        new_conv_ref[2] = projected_ref[1]
        new_coup_ref[0] = coup_ref[1]
        new_coup_ref[1] = coup_ref[2]
        new_coup_ref[2] = pre_ref[...]
        key_value_ref[...] = qkv_ref[:, QH * HD :]

    width = blocks_ref.shape[2]
    for n in range(blocks_ref.shape[0]):
        logits_ref[:, n * width : (n + 1) * width] = blocks_ref[n].astype(jnp.float32)

    @pl.when(step == pl.num_programs(0) - 1)
    def _():
        copy.wait()


def finish(residual, blocks, state, conv_state, projected, coup_state, pre, qkv):
    count, each, vocab = blocks.shape
    steps = 4
    part = count // steps
    shaped = lambda a: jax.ShapeDtypeStruct(a.shape, a.dtype)
    whole = lambda shape: pl.BlockSpec(shape, lambda i: (0,) * len(shape))
    key_value = (qkv.shape[0], qkv.shape[1] - QH * HD)
    return pl.pallas_call(
        finish_kernel,
        grid=(steps,),
        in_specs=[
            whole(residual.shape),
            pl.BlockSpec((part, each, vocab), lambda i: (i, 0, 0)),
            pl.BlockSpec(memory_space=pl.ANY),
            whole(conv_state.shape), whole(projected.shape), whole(coup_state.shape),
            whole(pre.shape), whole(qkv.shape),
        ],
        out_specs=[
            whole(residual.shape),
            pl.BlockSpec((each, part * vocab), lambda i: (0, i)),
            pl.BlockSpec(memory_space=pltpu.HBM),
            whole(conv_state.shape), whole(coup_state.shape), whole(key_value),
        ],
        out_shape=[
            shaped(residual),
            jax.ShapeDtypeStruct((each, count * vocab), jnp.float32),
            shaped(state), shaped(conv_state), shaped(coup_state),
            jax.ShapeDtypeStruct(key_value, qkv.dtype),
        ],
        scratch_shapes=[pltpu.SemaphoreType.DMA((1,))],
        compiler_params=pltpu.CompilerParams(vmem_limit_bytes=8 << 20),
    )(residual, blocks, state, conv_state, projected, coup_state, pre, qkv)


def body(
    residual,
    cache_lengths,
    input_gain,
    inner_weight,
    step_weight,
    step_bias,
    decay_log,
    skip_gain,
    conv_weight,
    conv_state,
    coupling_weight,
    coupling_conv,
    coupling_state,
    scan_state,
    mixer_gain,
    attention_weight,
    sink_cache,
    window_cache,
    mamba_out,
    attention_out,
    final_gain,
    output_head,
):
    row_count = residual.shape[0]
    local_units = inner_weight.shape[2]
    swap = lambda array: jnp.transpose(array, (1, 0, 2))
    coup_state = swap(coupling_state)
    normed, coupling_pre, qkv_rows, coupling_all, step_size, decay_rate = entry(
        step_bias, decay_log, residual, input_gain, attention_weight, coupling_weight,
        coupling_conv, coup_state, step_weight.T,
    )
    projected = jnp.einsum(
        "rd,dtc->trc", normed, inner_weight, preferred_element_type=jnp.float32
    ).astype(jnp.bfloat16)
    conv_rows_first = swap(conv_state)
    fresh_residual, fresh_state, blocks = joint(
        cache_lengths, skip_gain, qkv_rows, sink_cache, window_cache,
        scan_state.reshape(row_count, local_units, NS), coupling_all, projected, conv_weight,
        conv_rows_first, step_size, decay_rate, mixer_gain, mamba_out, attention_out, residual,
        final_gain, output_head,
    )
    new_residual, logits, new_state, new_conv, new_coup, new_key_value = finish(
        fresh_residual, blocks, fresh_state, conv_rows_first, projected, coup_state, coupling_pre,
        qkv_rows,
    )
    new_conv_state = swap(new_conv)
    new_coupling_state = swap(new_coup)
    new_scan_state = new_state.reshape(scan_state.shape)
    return (new_residual, logits, new_scan_state, new_conv_state, new_coupling_state, new_key_value)


def solution(mesh):
    return jax.shard_map(
        body,
        mesh=mesh,
        in_specs=(
            P("req", None),
            P("req"),
            P(),
            P(None, None, "tp"),
            P(None, "tp"),
            P("tp"),
            P("tp"),
            P("tp"),
            P(None, "tp"),
            P("req", None, "tp"),
            P(None, "tp"),
            P(None, "tp"),
            P("req", None, "tp"),
            P("req", "tp", None, None),
            P("tp"),
            P(None, "tp"),
            P("req", None, None),
            P("req", "tp", None),
            P("tp", None),
            P("tp", None),
            P(),
            P(None, ("req", "tp")),
        ),
        out_specs=(
            P("req", "tp"),
            P(("req", "tp"), None),
            P("req", "tp", None, None),
            P("req", None, "tp"),
            P("req", None, "tp"),
            P("req", None),
        ),
        check_vma=False,
    )
```

```python
import functools

import jax
import jax.numpy as jnp
from jax import lax
from jax.experimental import pallas as pl
from jax.experimental.pallas import tpu as pltpu
from jax.sharding import PartitionSpec as P

MH = 24
MP = 64
NS = 256
QH = 8
KVH = 2
HD = 128
WIN = 1024
SINK = 4
BR = 8

EPSILON = 1e-05
NEG_BIG = -1e30
MESH = pl.DeviceIdType.MESH
NT = (((1,), (1,)), ((), ()))


def norm_rows(values, gain):
    widened = values.astype(jnp.float32)
    mean_sq = jnp.mean(widened * widened, axis=-1, keepdims=True)
    return (widened * lax.rsqrt(mean_sq + EPSILON) * gain).astype(jnp.bfloat16)


def silu(v):
    return v / (1.0 + jnp.exp(-v))


def conv_rows(old, fresh, taps_ref):
    steps = [row.astype(jnp.float32) for row in (*old, fresh)]
    taps = taps_ref[...].astype(jnp.float32)
    mixed = steps[0] * taps[0:1]
    for k in range(1, 4):
        mixed = mixed + steps[k] * taps[k : k + 1]
    return silu(mixed)


def by_head(ref, g, shape):
    lane = lax.broadcasted_iota(jnp.int32, shape, 1)
    return jnp.where(lane < MP, ref[2 * g], ref[2 * g + 1])


def entry_kernel(
    tp_size, bias_src, log_src, residual_src, gain_src, attention_src, coupling_src, taps_src,
    state_src, step_weight_src, normed_ref, pre_ref, qkv_ref, coup_ref, step_ref, decay_ref,
    residual_ref, gain_ref, attention_ref, coupling_ref, taps_ref,
    state_ref, step_weight_ref, bias_ref, log_ref, load_sem, qkv_s, qkv_r, coup_s, coup_r,
):
    r = lax.axis_index("req")
    t = lax.axis_index("tp")
    peers = [lax.rem(t + k, tp_size) for k in range(tp_size)]
    barrier = pltpu.get_barrier_semaphore()
    for k in range(1, tp_size):
        pl.semaphore_signal(barrier, inc=1, device_id=(r, peers[k]), device_id_type=MESH)
    sources = [
        residual_src, gain_src, attention_src, coupling_src, taps_src, state_src, step_weight_src,
        bias_src, log_src,
    ]
    places = [
        residual_ref, gain_ref, attention_ref, coupling_ref, taps_ref, state_ref, step_weight_ref,
        bias_ref, log_ref,
    ]
    loads = [
        pltpu.make_async_copy(src, dst, load_sem.at[n])
        for n, (src, dst) in enumerate(zip(sources, places))
    ]
    for load in loads:
        load.start()
    loads[0].wait()
    loads[1].wait()
    normed = norm_rows(residual_ref[...], gain_ref[...])
    normed_ref[...] = normed
    copies = []

    def share(out_ref, value, ssem, rsem):
        width = value.shape[1]
        cols = pl.ds(pl.multiple_of(t * width, 128), width)
        out_ref[:, cols] = value
        for k in range(1, tp_size):
            copy = pltpu.make_async_remote_copy(
                src_ref=out_ref.at[:, cols], dst_ref=out_ref.at[:, cols], send_sem=ssem.at[k],
                recv_sem=rsem.at[k], device_id=(r, peers[k]), device_id_type=MESH,
            )
            copy.start()
            copies.append(copy)

    loads[2].wait()
    qkv = jnp.dot(normed, attention_ref[...], preferred_element_type=jnp.float32)
    pl.semaphore_wait(barrier, tp_size - 1)
    share(qkv_ref, qkv.astype(jnp.bfloat16), qkv_s, qkv_r)
    for load in loads[3:]:
        load.wait()
    pre = jnp.dot(normed, coupling_ref[...], preferred_element_type=jnp.float32).astype(jnp.bfloat16)
    pre_ref[...] = pre
    share(coup_ref, conv_rows([state_ref[k] for k in range(3)], pre, taps_ref).astype(jnp.bfloat16), coup_s, coup_r)
    steps = (
        lax.dot_general(normed, step_weight_ref[...], NT, preferred_element_type=jnp.float32)
        .astype(jnp.bfloat16)
        .astype(jnp.float32)
    )
    shape = (normed.shape[0], 2 * MP)
    for g in range(steps.shape[1] // 2):
        lane = lax.broadcasted_iota(jnp.int32, shape, 1)
        v = jnp.where(lane < MP, steps[:, 2 * g : 2 * g + 1], steps[:, 2 * g + 1 : 2 * g + 2])
        v = v + by_head(bias_ref, g, shape)
        size = jnp.maximum(v, 0.0) + jnp.log1p(jnp.exp(-jnp.abs(v)))
        step_ref[:, g * 2 * MP : (g + 1) * 2 * MP] = size
        decay_ref[:, g * 2 * MP : (g + 1) * 2 * MP] = jnp.exp(
            -size * jnp.exp(by_head(log_ref, g, shape))
        )
    for copy in copies:
        copy.wait()


def entry(bias, decay_log, residual, gain, attention_weight, coupling_weight, taps, state, step_weight):
    tp_size = lax.axis_size("tp")
    rows, model = residual.shape
    units = bias.shape[0] * MP
    vmem = pl.BlockSpec(memory_space=pltpu.VMEM)
    hbm = pl.BlockSpec(memory_space=pltpu.HBM)
    dma = pltpu.SemaphoreType.DMA((tp_size,))
    operands = (residual, gain[None], attention_weight, coupling_weight, taps, state, step_weight)
    levels = (bias, decay_log)
    shaped = jax.ShapeDtypeStruct
    return pl.pallas_call(
        functools.partial(entry_kernel, tp_size),
        in_specs=[hbm] * 9,
        out_specs=[vmem] * 6,
        out_shape=[
            shaped((rows, model), jnp.bfloat16),
            shaped((rows, coupling_weight.shape[1]), jnp.bfloat16),
            shaped((rows, attention_weight.shape[1] * tp_size), jnp.bfloat16),
            shaped((rows, coupling_weight.shape[1] * tp_size), jnp.bfloat16),
            shaped((rows, units), jnp.float32),
            shaped((rows, units), jnp.float32),
        ],
        scratch_shapes=[pltpu.VMEM(a.shape, a.dtype) for a in operands]
        + [pltpu.SMEM(a.shape, a.dtype) for a in levels]
        + [pltpu.SemaphoreType.DMA((len(operands) + len(levels),))]
        + [dma] * 4,
        cost_estimate=pl.CostEstimate(flops=9_000_000_000, bytes_accessed=3_000_000, transcendentals=0),
        compiler_params=pltpu.CompilerParams(
            collective_id=0, has_side_effects=True, vmem_limit_bytes=8 << 20
        ),
    )(*map(keep, levels), *map(keep, operands))


def attend_block(
    i, len_ref, qkv_ref, sink_ref, window_ref, summed_ref, stats_ref, heads_scr, stat_scr, extra_scr
):
    half = KVH * HD
    group = QH // KVH
    t = lax.axis_index("tp")
    slots = window_ref.shape[1]
    qkv = qkv_ref[i]
    fresh = qkv[:, QH * HD :]

    for h in range(QH):
        heads_scr[pl.ds(h, BR, stride=QH), :] = qkv[:, h * HD : (h + 1) * HD].astype(jnp.float32)
    for j in range(BR):
        extra_scr[j * SINK : (j + 1) * SINK, :] = sink_ref[i * BR + j].astype(jnp.float32)
    extra_scr[BR * SINK : BR * SINK + BR, :] = fresh.astype(jnp.float32)
    extra_scr[BR * SINK + BR :, :] = jnp.zeros_like(extra_scr[BR * SINK + BR :, :])
    extra = extra_scr[...].astype(jnp.bfloat16)
    head_row = lax.broadcasted_iota(jnp.int32, (BR * QH, HD), 0) % QH
    lane = lax.broadcasted_iota(jnp.int32, (BR * QH, HD), 1)
    first_half = head_row < group
    q = heads_scr[...]
    wide = jnp.concatenate([jnp.where(first_half, q, 0.0), jnp.where(first_half, 0.0, q)], axis=1)
    block = lambda array, j: array[j * QH : (j + 1) * QH]
    slot = t * slots + lax.broadcasted_iota(jnp.int32, (QH, slots), 1)
    lives, scores = [], []
    for j in range(BR):
        last = len_ref[i * BR + j] - 1
        back = jnp.bitwise_and(last - slot, WIN - 1)
        lives.append((last - back >= SINK) & (back != WIN - 1))
        raw = lax.dot_general(
            block(wide, j).astype(jnp.bfloat16), window_ref[i * BR + j, :, :half], NT,
            preferred_element_type=jnp.float32,
        )
        scores.append(jnp.where(lives[j], raw * HD ** (-0.5), NEG_BIG))
    s1 = jnp.concatenate(scores, axis=0)
    s2 = lax.dot_general(
        wide.astype(jnp.bfloat16), extra[:, :half], NT, preferred_element_type=jnp.float32
    ) * HD ** (-0.5)
    col = lax.broadcasted_iota(jnp.int32, s2.shape, 1)
    owner = lax.broadcasted_iota(jnp.int32, s2.shape, 0) // QH
    live2 = (jnp.where(col < BR * SINK, col // SINK, col - BR * SINK) == owner) & (t == 0)
    s2 = jnp.where(live2, s2, NEG_BIG)
    peak = jnp.maximum(jnp.max(s1, axis=1, keepdims=True), jnp.max(s2, axis=1, keepdims=True))
    w1 = jnp.exp(s1 - peak)
    w1 = jnp.concatenate([jnp.where(lives[j], block(w1, j), 0.0) for j in range(BR)], axis=0)
    w2 = jnp.where(live2, jnp.exp(s2 - peak), 0.0)
    total = jnp.sum(w1, axis=1, keepdims=True) + jnp.sum(w2, axis=1, keepdims=True)
    acc = jnp.concatenate(
        [
            jnp.dot(
                block(w1, j).astype(jnp.bfloat16), window_ref[i * BR + j, :, half:],
                preferred_element_type=jnp.float32,
            )
            for j in range(BR)
        ],
        axis=0,
    ) + jnp.dot(w2.astype(jnp.bfloat16), extra[:, half:], preferred_element_type=jnp.float32)
    heads_scr[...] = jnp.where(first_half, acc[:, :HD], acc[:, HD:])
    stat_scr[...] = jnp.where(lane == head_row, peak, 0.0) + jnp.where(
        lane == head_row + QH, total, 0.0
    )
    stats_ref[i] = functools.reduce(
        jnp.add, [stat_scr[pl.ds(h, BR, stride=QH), :] for h in range(QH)]
    )
    per_chunk = summed_ref.shape[3] // HD
    for h in range(QH):
        summed_ref[h // per_chunk, i, :, (h % per_chunk) * HD : (h % per_chunk + 1) * HD] = heads_scr[
            pl.ds(h, BR, stride=QH), :
        ].astype(jnp.bfloat16)


def scan_block(
    i, skip_ref, state_ref, coup_ref, projected_ref, taps_ref, conv_state_ref, step_ref, decay_ref,
    gated_ref, square_ref, step_x_ref,
):
    units = step_ref.shape[2]
    coup = coup_ref[i]
    out_rows = coup[:, NS:]
    in_f32 = coup[:, :NS].astype(jnp.float32)
    gate = projected_ref[0, i].astype(jnp.float32)
    x_pre = projected_ref[1, i]
    x = conv_rows([conv_state_ref[k, i] for k in range(3)], x_pre, taps_ref)
    step_x = step_ref[i] * x
    step_x_ref[i] = step_x
    decay = decay_ref[i]
    both = jnp.sum(in_f32 * out_rows.astype(jnp.float32), axis=1, keepdims=True)
    read_rows = []
    for j in range(BR):
        state = state_ref[i * BR + j]
        read_rows.append(
            lax.dot_general(out_rows, state, NT, preferred_element_type=jnp.float32)[j : j + 1, :]
        )
    readout = decay * jnp.concatenate(read_rows, axis=0) + step_x * both
    skip = jnp.concatenate(
        [by_head(skip_ref, g, (BR, 2 * MP)) for g in range(units // (2 * MP))], axis=1
    )
    gated = (readout + skip * x) * silu(gate)
    gated_ref[i] = gated
    square_ref[i] = jnp.broadcast_to(
        jnp.sum(gated * gated, axis=1, keepdims=True), square_ref.shape[1:]
    )


def update_block(i, state_ref, coup_ref, step_x_ref, decay_ref, new_state_ref):
    in_f32 = coup_ref[i][:, :NS].astype(jnp.float32)
    step_x_t = step_x_ref[i].T
    decay_t = decay_ref[i].T
    for j in range(BR):
        new_state_ref[i * BR + j] = (
            decay_t[:, j : j + 1] * state_ref[i * BR + j].astype(jnp.float32)
            + step_x_t[:, j : j + 1] * in_f32[j : j + 1, :]
        ).astype(jnp.bfloat16)


def ahead(array):
    return pltpu.with_memory_space_constraint(array, pltpu.VMEM)


def keep(array):
    return pltpu.with_memory_space_constraint(array, pltpu.HBM)


def other(index, k, size):
    total, bit = 0, 1
    while bit < size:
        a, b = lax.rem(lax.div(index, bit), 2), lax.rem(lax.div(k, bit), 2)
        total = total + bit * (a + b - 2 * a * b)
        bit *= 2
    return total


def joint_kernel(
    tp_size, req_size, len_ref, skip_ref, qkv_ref, sink_ref, window_ref, state_ref, coup_ref,
    projected_ref, taps_ref, conv_state_ref, step_ref, decay_ref, mixer_gain_ref, residual_ref,
    final_gain_ref, mamba_out_ref, attention_out_ref, head_ref, new_residual_ref, new_state_ref,
    logits_ref, heads_scr, stat_scr, extra_scr, summed_ref, stats_ref, gated_ref, square_ref,
    step_x_ref, square_buf, scan_out, scan_buf, mamba_buf, attention_buf, head_buf, sum_buf, stat_buf, part_out, part_buf, gather, final_buf,
    logit_out, square_s, square_r, scan_s, scan_r, sum_s, sum_r, stat_s, stat_r, part_s, part_r, gat_s, gat_r, log_s, log_r, load_sem,
):
    r = lax.axis_index("req")
    t = lax.axis_index("tp")
    rows = residual_ref.shape[0]
    blocks = rows // BR
    width = new_residual_ref.shape[1]
    peers = [other(t, q, tp_size) for q in range(tp_size)]
    reqs = [other(r, k, req_size) for k in range(req_size)]
    barrier = pltpu.get_barrier_semaphore()
    for q in range(1, tp_size):
        pl.semaphore_signal(barrier, inc=1, device_id=(r, peers[q]), device_id_type=MESH)
    for k in range(1, req_size):
        pl.semaphore_signal(barrier, inc=1, device_id=(reqs[k], t), device_id_type=MESH)
    load_mamba = pltpu.make_async_copy(mamba_out_ref, mamba_buf, load_sem.at[1])
    load_attention = pltpu.make_async_copy(attention_out_ref, attention_buf, load_sem.at[2])
    load_head = pltpu.make_async_copy(head_ref, head_buf, load_sem.at[3])
    for load in (load_mamba, load_attention, load_head):
        load.start()

    def attend(i, carry):
        attend_block(
            i, len_ref, qkv_ref, sink_ref, window_ref, summed_ref, stats_ref, heads_scr, stat_scr,
            extra_scr,
        )
        return carry

    lax.fori_loop(0, blocks, attend, 0)
    pl.semaphore_wait(barrier, tp_size + req_size - 2)

    def send(src, dst, ssem, rsem, where):
        copy = pltpu.make_async_remote_copy(
            src_ref=src, dst_ref=dst, send_sem=ssem, recv_sem=rsem,
            device_id=where, device_id_type=MESH,
        )
        copy.start()
        return copy

    first = []
    for q in reversed(range(1, tp_size)):
        where = (r, peers[q])
        first.append(send(stats_ref, stat_buf.at[q], stat_s.at[q], stat_r.at[q], where))
        first.append(send(summed_ref.at[peers[q]], sum_buf.at[q], sum_s.at[q], sum_r.at[q], where))

    def scan(i, carry):
        scan_block(
            i, skip_ref, state_ref, coup_ref, projected_ref, taps_ref, conv_state_ref, step_ref,
            decay_ref, gated_ref, square_ref, step_x_ref,
        )
        return carry

    lax.fori_loop(0, blocks, scan, 0)
    gated = gated_ref[...].reshape(rows, gated_ref.shape[2])
    mamba = (gated * mixer_gain_ref[...][None]).astype(jnp.bfloat16)
    columns = lambda p: pl.ds(pl.multiple_of(p * width, 128), width)
    load_mamba.wait()

    def unscaled(q):
        return jnp.dot(mamba, mamba_buf[:, columns(peers[q])], preferred_element_type=jnp.float32)

    between = []
    for q in reversed(range(1, tp_size)):
        where = (r, peers[q])
        between.append(send(square_ref, square_buf.at[q], square_s.at[q], square_r.at[q], where))
        scan_out[q] = unscaled(q).astype(jnp.bfloat16)
        between.append(send(scan_out.at[q], scan_buf.at[q], scan_s.at[q], scan_r.at[q], where))
    scanned = unscaled(0)
    load_attention.wait()
    for copy in first:
        copy.wait()
    flat = lambda array: array.astype(jnp.float32).reshape(rows, array.shape[2])
    stats = [flat(stats_ref[...])] + [flat(stat_buf[q]) for q in range(1, tp_size)]
    sums = [flat(summed_ref[t])] + [flat(sum_buf[q]) for q in range(1, tp_size)]
    lane = lax.broadcasted_iota(jnp.int32, (rows, 128), 1)
    local_heads = QH // tp_size
    pieces = []
    for hl in range(local_heads):
        h = t * local_heads + hl
        peaks = [jnp.sum(jnp.where(lane == h, s, 0.0), axis=1, keepdims=True) for s in stats]
        totals = [jnp.sum(jnp.where(lane == h + QH, s, 0.0), axis=1, keepdims=True) for s in stats]
        top = functools.reduce(jnp.maximum, peaks)
        scales = [jnp.exp(p - top) for p in peaks]
        below = functools.reduce(jnp.add, [a * b for a, b in zip(scales, totals)])
        above = functools.reduce(
            jnp.add, [a * b[:, hl * HD : (hl + 1) * HD] for a, b in zip(scales, sums)]
        )
        pieces.append((above / below).astype(jnp.bfloat16))
    attended = jnp.concatenate(pieces, axis=1)

    def partial(q):
        return jnp.dot(
            attended, attention_buf[:, columns(peers[q])], preferred_element_type=jnp.float32
        )

    second = {}
    for q in reversed(range(1, tp_size)):
        part_out[q] = partial(q).astype(jnp.bfloat16)
        second[q] = send(part_out.at[q], part_buf.at[q], part_s.at[q], part_r.at[q], (r, peers[q]))
    mixed = residual_ref[:, columns(t)].astype(jnp.float32) + partial(0)
    for copy in between:
        copy.wait()
    square = flat(square_ref[...])[:, :1]
    for q in range(1, tp_size):
        square = square + flat(square_buf[q])[:, :1]
        scanned = scanned + scan_buf[q].astype(jnp.float32)
    mixed = mixed + scanned * lax.rsqrt(square / (MH * MP) + EPSILON)
    for q in range(1, tp_size):
        second[q].wait()
        mixed = mixed + part_buf[q].astype(jnp.float32)
    fresh = mixed.astype(jnp.bfloat16)
    new_residual_ref[...] = fresh
    gather[0, 0] = fresh

    half = req_size // 2
    far_groups = list(range(half, req_size))
    near_groups = list(range(1, half))

    def move(k, src, dst, where):
        return pltpu.make_async_remote_copy(
            src_ref=gather.at[k if src else 0, src - 1 if src else 0], dst_ref=gather.at[k, dst],
            send_sem=gat_s.at[k, dst], recv_sem=gat_r.at[k, dst],
            device_id=where, device_id_type=MESH,
        )

    along = lambda k: move(k, 0, 0, (other(r, k, req_size), t))
    over = lambda k: move(k, 1, 2, (r, peers[2]))
    near = lambda k: move(k, 1, 1, (r, peers[1]))
    far = lambda k: move(k, 3, 3, (r, peers[1]))

    def spread(k):
        if k:
            along(k).wait_recv()
        over(k).start()
        near(k).start()

    def pair_up(k):
        over(k).wait_recv()
        far(k).start()

    along(half).start()
    for k in far_groups[1:] + near_groups:
        along(k).start()
    spread(half)
    spread(0)
    spread(half + 1)
    for k in near_groups:
        spread(k)
    pair_up(half)
    for k in far_groups[2:3]:
        spread(k)

    vocab = head_buf.shape[1]
    tile = min(1024, vocab)
    each = rows // tp_size
    source = r * tp_size + t

    def logits_to(k, q):
        return pltpu.make_async_remote_copy(
            src_ref=logit_out.at[k, peers[q]], dst_ref=logits_ref.at[source],
            send_sem=log_s.at[k, q], recv_sem=log_r.at[k, q],
            device_id=(other(r, k, req_size), peers[q]), device_id_type=MESH,
        )

    own = pltpu.make_async_copy(logit_out.at[0, t], logits_ref.at[source], load_sem.at[0])
    def group_at(n):
        late = lax.div(n, half)
        return (1 - late) * (n + half) + late * (req_size - 1 - n)

    load_head.wait()

    def project(n, carry):
        k = group_at(n)
        near(k).wait_recv()
        far(k).wait_recv()
        squares = jnp.zeros((rows, width), jnp.float32)
        for i in range(tp_size):
            value = gather[k, i].astype(jnp.float32)
            squares = squares + value * value
        mean = jnp.sum(squares, axis=1, keepdims=True) / (width * tp_size)
        scale = lax.rsqrt(mean + EPSILON)
        for i in range(tp_size):
            cols = columns(peers[i])
            final_buf[:, cols] = (
                gather[k, i].astype(jnp.float32) * scale * final_gain_ref[:, cols]
            ).astype(jnp.bfloat16)

        @pl.when(n + 1 < req_size)
        def _():
            pair_up(group_at(n + 1))

        def head_tile(c, carry):
            cols = pl.ds(pl.multiple_of(c * tile, 128), tile)
            part = jnp.dot(
                final_buf[...], head_buf[:, cols], preferred_element_type=jnp.float32
            )
            for q in range(tp_size):
                logit_out[k, q, :, cols] = part[q * each : (q + 1) * each, :].astype(jnp.bfloat16)
            return carry

        lax.fori_loop(0, vocab // tile, head_tile, 0)
        for q in reversed(range(1, tp_size)):
            logits_to(k, q).start()

        @pl.when(n != req_size - 1)
        def _():
            logits_to(k, 0).start()

        @pl.when(n == 0)
        def _():
            for later in far_groups[3:]:
                spread(later)

        @pl.when(n == req_size - 1)
        def _():
            own.start()

        return carry

    lax.fori_loop(0, req_size, project, 0)
    def update(i, carry):
        update_block(i, state_ref, coup_ref, step_x_ref, decay_ref, new_state_ref)
        return carry

    lax.fori_loop(0, blocks, update, 0)
    own.wait()

    def close(n, carry):
        k = group_at(n)
        for q in reversed(range(1, tp_size)):
            logits_to(k, q).wait()
        over(k).wait_send()
        near(k).wait_send()
        far(k).wait_send()

        @pl.when(n != req_size - 1)
        def _():
            logits_to(k, 0).wait()
            along(k).wait_send()

        return carry

    lax.fori_loop(0, req_size, close, 0)


def joint(
    lengths, skip, qkv, sink, window, state, coup, projected, taps, conv_state, step, decay,
    mixer_gain, mamba_out, attention_out, residual, final_gain, output_head,
):
    tp_size = lax.axis_size("tp")
    req_size = lax.axis_size("req")
    rows, model = residual.shape
    units = step.shape[1]
    blocks = rows // BR
    width = model // tp_size
    chunk = QH * HD // tp_size
    each = rows // tp_size
    vocab = output_head.shape[1]

    def split(a):
        at = a.ndim - 2
        return a.reshape(a.shape[:at] + (blocks, BR) + a.shape[at + 1 :])

    dma = lambda *shape: pltpu.SemaphoreType.DMA(shape)
    vmem = pl.BlockSpec(memory_space=pltpu.VMEM)
    smem = pl.BlockSpec(memory_space=pltpu.SMEM)
    hbm = pl.BlockSpec(memory_space=pltpu.HBM)
    return pl.pallas_call(
        functools.partial(joint_kernel, tp_size, req_size),
        in_specs=[smem] * 2 + [vmem] * 13 + [hbm] * 3,
        out_specs=[vmem, vmem, hbm],
        out_shape=[
            jax.ShapeDtypeStruct((rows, width), jnp.bfloat16),
            jax.ShapeDtypeStruct(state.shape, jnp.bfloat16),
            jax.ShapeDtypeStruct((req_size * tp_size, each, vocab), jnp.bfloat16),
        ],
        scratch_shapes=[
            pltpu.VMEM((BR * QH, HD), jnp.float32),
            pltpu.VMEM((BR * QH, HD), jnp.float32),
            pltpu.VMEM((BR * QH, 2 * KVH * HD), jnp.float32),
            pltpu.VMEM((tp_size, blocks, BR, chunk), jnp.bfloat16),
            pltpu.VMEM((blocks, BR, 128), jnp.float32),
            pltpu.VMEM((blocks, BR, units), jnp.float32),
            pltpu.VMEM((blocks, BR, 128), jnp.float32),
            pltpu.VMEM((blocks, BR, units), jnp.float32),
            pltpu.VMEM((tp_size, blocks, BR, 128), jnp.float32),
            pltpu.VMEM((tp_size, rows, width), jnp.bfloat16),
            pltpu.VMEM((tp_size, rows, width), jnp.bfloat16),
            pltpu.VMEM(mamba_out.shape, jnp.bfloat16),
            pltpu.VMEM(attention_out.shape, jnp.bfloat16),
            pltpu.VMEM(output_head.shape, jnp.bfloat16),
            pltpu.VMEM((tp_size, blocks, BR, chunk), jnp.bfloat16),
            pltpu.VMEM((tp_size, blocks, BR, 128), jnp.float32),
            pltpu.VMEM((tp_size, rows, width), jnp.bfloat16),
            pltpu.VMEM((tp_size, rows, width), jnp.bfloat16),
            pltpu.VMEM((req_size, tp_size, rows, width), jnp.bfloat16),
            pltpu.VMEM((rows, model), jnp.bfloat16),
            pltpu.VMEM((req_size, tp_size, each, vocab), jnp.bfloat16),
            dma(tp_size), dma(tp_size), dma(tp_size), dma(tp_size), dma(tp_size), dma(tp_size),
            dma(tp_size), dma(tp_size), dma(tp_size), dma(tp_size),
            dma(req_size, tp_size), dma(req_size, tp_size), dma(req_size, tp_size),
            dma(req_size, tp_size), dma(4),
        ],
        cost_estimate=pl.CostEstimate(
            flops=40_000_000_000, bytes_accessed=30_000_000, transcendentals=0
        ),
        compiler_params=pltpu.CompilerParams(
            collective_id=1, has_side_effects=True, vmem_limit_bytes=24 << 20
        ),
    )(
        lengths, skip, split(qkv), sink, ahead(window), ahead(state), split(coup), split(projected),
        taps, split(conv_state), split(step), split(decay), mixer_gain, residual, final_gain[None],
        keep(mamba_out), keep(attention_out), keep(output_head),
    )


def finish_kernel(
    residual_ref, blocks_ref, state_ref, conv_ref, projected_ref, coup_ref, pre_ref, qkv_ref,
    new_residual_ref, logits_ref, new_state_ref, new_conv_ref, new_coup_ref, key_value_ref, sem,
):
    copy = pltpu.make_async_copy(state_ref, new_state_ref, sem.at[0])
    step = pl.program_id(0)

    @pl.when(step == 0)
    def _():
        copy.start()
        new_residual_ref[...] = residual_ref[...]
        new_conv_ref[0] = conv_ref[1]
        new_conv_ref[1] = conv_ref[2]
        new_conv_ref[2] = projected_ref[1]
        new_coup_ref[0] = coup_ref[1]
        new_coup_ref[1] = coup_ref[2]
        new_coup_ref[2] = pre_ref[...]
        key_value_ref[...] = qkv_ref[:, QH * HD :]

    width = blocks_ref.shape[2]
    for n in range(blocks_ref.shape[0]):
        logits_ref[:, n * width : (n + 1) * width] = blocks_ref[n].astype(jnp.float32)

    @pl.when(step == pl.num_programs(0) - 1)
    def _():
        copy.wait()


def finish(residual, blocks, state, conv_state, projected, coup_state, pre, qkv):
    count, each, vocab = blocks.shape
    steps = 2
    part = count // steps
    shaped = lambda a: jax.ShapeDtypeStruct(a.shape, a.dtype)
    whole = lambda shape: pl.BlockSpec(shape, lambda i: (0,) * len(shape))
    key_value = (qkv.shape[0], qkv.shape[1] - QH * HD)
    return pl.pallas_call(
        finish_kernel,
        grid=(steps,),
        in_specs=[
            whole(residual.shape),
            pl.BlockSpec((part, each, vocab), lambda i: (i, 0, 0)),
            pl.BlockSpec(memory_space=pl.ANY),
            whole(conv_state.shape), whole(projected.shape), whole(coup_state.shape),
            whole(pre.shape), whole(qkv.shape),
        ],
        out_specs=[
            whole(residual.shape),
            pl.BlockSpec((each, part * vocab), lambda i: (0, i)),
            pl.BlockSpec(memory_space=pltpu.HBM),
            whole(conv_state.shape), whole(coup_state.shape), whole(key_value),
        ],
        out_shape=[
            shaped(residual),
            jax.ShapeDtypeStruct((each, count * vocab), jnp.float32),
            shaped(state), shaped(conv_state), shaped(coup_state),
            jax.ShapeDtypeStruct(key_value, qkv.dtype),
        ],
        scratch_shapes=[pltpu.SemaphoreType.DMA((1,))],
        compiler_params=pltpu.CompilerParams(vmem_limit_bytes=8 << 20),
    )(residual, blocks, state, conv_state, projected, coup_state, pre, qkv)


def body(
    residual,
    cache_lengths,
    input_gain,
    inner_weight,
    step_weight,
    step_bias,
    decay_log,
    skip_gain,
    conv_weight,
    conv_state,
    coupling_weight,
    coupling_conv,
    coupling_state,
    scan_state,
    mixer_gain,
    attention_weight,
    sink_cache,
    window_cache,
    mamba_out,
    attention_out,
    final_gain,
    output_head,
):
    row_count = residual.shape[0]
    local_units = inner_weight.shape[2]
    swap = lambda array: jnp.transpose(array, (1, 0, 2))
    coup_state = swap(coupling_state)
    normed, coupling_pre, qkv_rows, coupling_all, step_size, decay_rate = entry(
        step_bias, decay_log, residual, input_gain, attention_weight, coupling_weight,
        coupling_conv, coup_state, step_weight.T,
    )
    projected = jnp.einsum(
        "rd,dtc->trc", normed, inner_weight, preferred_element_type=jnp.float32
    ).astype(jnp.bfloat16)
    conv_rows_first = swap(conv_state)
    fresh_residual, fresh_state, blocks = joint(
        cache_lengths, skip_gain, qkv_rows, sink_cache, window_cache,
        scan_state.reshape(row_count, local_units, NS), coupling_all, projected, conv_weight,
        conv_rows_first, step_size, decay_rate, mixer_gain, mamba_out, attention_out, residual,
        final_gain, output_head,
    )
    new_residual, logits, new_state, new_conv, new_coup, new_key_value = finish(
        fresh_residual, blocks, fresh_state, conv_rows_first, projected, coup_state, coupling_pre,
        qkv_rows,
    )
    new_conv_state = swap(new_conv)
    new_coupling_state = swap(new_coup)
    new_scan_state = new_state.reshape(scan_state.shape)
    return (new_residual, logits, new_scan_state, new_conv_state, new_coupling_state, new_key_value)


def solution(mesh):
    return jax.shard_map(
        body,
        mesh=mesh,
        in_specs=(
            P("req", None),
            P("req"),
            P(),
            P(None, None, "tp"),
            P(None, "tp"),
            P("tp"),
            P("tp"),
            P("tp"),
            P(None, "tp"),
            P("req", None, "tp"),
            P(None, "tp"),
            P(None, "tp"),
            P("req", None, "tp"),
            P("req", "tp", None, None),
            P("tp"),
            P(None, "tp"),
            P("req", None, None),
            P("req", "tp", None),
            P("tp", None),
            P("tp", None),
            P(),
            P(None, ("req", "tp")),
        ),
        out_specs=(
            P("req", "tp"),
            P(("req", "tp"), None),
            P("req", "tp", None, None),
            P("req", None, "tp"),
            P("req", None, "tp"),
            P("req", None),
        ),
        check_vma=False,
    )
```

```python
import functools

import jax
import jax.numpy as jnp
from jax import lax
from jax.experimental import pallas as pl
from jax.experimental.pallas import tpu as pltpu
from jax.sharding import PartitionSpec as P

MH = 24
MP = 64
NS = 256
QH = 8
KVH = 2
HD = 128
WIN = 1024
SINK = 4
BR = 8

EPSILON = 1e-05
NEG_BIG = -1e30
MESH = pl.DeviceIdType.MESH
NT = (((1,), (1,)), ((), ()))


def norm_rows(values, gain):
    widened = values.astype(jnp.float32)
    mean_sq = jnp.mean(widened * widened, axis=-1, keepdims=True)
    return (widened * lax.rsqrt(mean_sq + EPSILON) * gain).astype(jnp.bfloat16)


def silu(v):
    return v / (1.0 + jnp.exp(-v))


def conv_rows(old, fresh, taps_ref):
    steps = [row.astype(jnp.float32) for row in (*old, fresh)]
    taps = taps_ref[...].astype(jnp.float32)
    mixed = steps[0] * taps[0:1]
    for k in range(1, 4):
        mixed = mixed + steps[k] * taps[k : k + 1]
    return silu(mixed)


def by_head(ref, g, shape):
    lane = lax.broadcasted_iota(jnp.int32, shape, 1)
    return jnp.where(lane < MP, ref[2 * g], ref[2 * g + 1])


def entry_kernel(
    tp_size, bias_src, log_src, residual_src, gain_src, attention_src, coupling_src, taps_src,
    state_src, step_weight_src, normed_ref, pre_ref, qkv_ref, coup_ref, step_ref, decay_ref,
    residual_ref, gain_ref, attention_ref, coupling_ref, taps_ref,
    state_ref, step_weight_ref, bias_ref, log_ref, load_sem, qkv_s, qkv_r, coup_s, coup_r,
):
    r = lax.axis_index("req")
    t = lax.axis_index("tp")
    peers = [lax.rem(t + k, tp_size) for k in range(tp_size)]
    barrier = pltpu.get_barrier_semaphore()
    for k in range(1, tp_size):
        pl.semaphore_signal(barrier, inc=1, device_id=(r, peers[k]), device_id_type=MESH)
    sources = [
        residual_src, gain_src, attention_src, coupling_src, taps_src, state_src, step_weight_src,
        bias_src, log_src,
    ]
    places = [
        residual_ref, gain_ref, attention_ref, coupling_ref, taps_ref, state_ref, step_weight_ref,
        bias_ref, log_ref,
    ]
    loads = [
        pltpu.make_async_copy(src, dst, load_sem.at[n])
        for n, (src, dst) in enumerate(zip(sources, places))
    ]
    for load in loads:
        load.start()
    loads[0].wait()
    loads[1].wait()
    normed = norm_rows(residual_ref[...], gain_ref[...])
    normed_ref[...] = normed
    copies = []

    def share(out_ref, value, ssem, rsem):
        width = value.shape[1]
        cols = pl.ds(pl.multiple_of(t * width, 128), width)
        out_ref[:, cols] = value
        for k in range(1, tp_size):
            copy = pltpu.make_async_remote_copy(
                src_ref=out_ref.at[:, cols], dst_ref=out_ref.at[:, cols], send_sem=ssem.at[k],
                recv_sem=rsem.at[k], device_id=(r, peers[k]), device_id_type=MESH,
            )
            copy.start()
            copies.append(copy)

    loads[2].wait()
    qkv = jnp.dot(normed, attention_ref[...], preferred_element_type=jnp.float32)
    pl.semaphore_wait(barrier, tp_size - 1)
    share(qkv_ref, qkv.astype(jnp.bfloat16), qkv_s, qkv_r)
    for load in loads[3:]:
        load.wait()
    pre = jnp.dot(normed, coupling_ref[...], preferred_element_type=jnp.float32).astype(jnp.bfloat16)
    pre_ref[...] = pre
    share(coup_ref, conv_rows([state_ref[k] for k in range(3)], pre, taps_ref).astype(jnp.bfloat16), coup_s, coup_r)
    steps = (
        lax.dot_general(normed, step_weight_ref[...], NT, preferred_element_type=jnp.float32)
        .astype(jnp.bfloat16)
        .astype(jnp.float32)
    )
    shape = (normed.shape[0], 2 * MP)
    for g in range(steps.shape[1] // 2):
        lane = lax.broadcasted_iota(jnp.int32, shape, 1)
        v = jnp.where(lane < MP, steps[:, 2 * g : 2 * g + 1], steps[:, 2 * g + 1 : 2 * g + 2])
        v = v + by_head(bias_ref, g, shape)
        size = jnp.maximum(v, 0.0) + jnp.log1p(jnp.exp(-jnp.abs(v)))
        step_ref[:, g * 2 * MP : (g + 1) * 2 * MP] = size
        decay_ref[:, g * 2 * MP : (g + 1) * 2 * MP] = jnp.exp(
            -size * jnp.exp(by_head(log_ref, g, shape))
        )
    for copy in copies:
        copy.wait()


def entry(bias, decay_log, residual, gain, attention_weight, coupling_weight, taps, state, step_weight):
    tp_size = lax.axis_size("tp")
    rows, model = residual.shape
    units = bias.shape[0] * MP
    vmem = pl.BlockSpec(memory_space=pltpu.VMEM)
    hbm = pl.BlockSpec(memory_space=pltpu.HBM)
    dma = pltpu.SemaphoreType.DMA((tp_size,))
    operands = (residual, gain[None], attention_weight, coupling_weight, taps, state, step_weight)
    levels = (bias, decay_log)
    shaped = jax.ShapeDtypeStruct
    return pl.pallas_call(
        functools.partial(entry_kernel, tp_size),
        in_specs=[hbm] * 9,
        out_specs=[vmem] * 6,
        out_shape=[
            shaped((rows, model), jnp.bfloat16),
            shaped((rows, coupling_weight.shape[1]), jnp.bfloat16),
            shaped((rows, attention_weight.shape[1] * tp_size), jnp.bfloat16),
            shaped((rows, coupling_weight.shape[1] * tp_size), jnp.bfloat16),
            shaped((rows, units), jnp.float32),
            shaped((rows, units), jnp.float32),
        ],
        scratch_shapes=[pltpu.VMEM(a.shape, a.dtype) for a in operands]
        + [pltpu.SMEM(a.shape, a.dtype) for a in levels]
        + [pltpu.SemaphoreType.DMA((len(operands) + len(levels),))]
        + [dma] * 4,
        cost_estimate=pl.CostEstimate(flops=9_000_000_000, bytes_accessed=3_000_000, transcendentals=0),
        compiler_params=pltpu.CompilerParams(
            collective_id=0, has_side_effects=True, vmem_limit_bytes=8 << 20
        ),
    )(*map(keep, levels), *map(keep, operands))


def attend_block(
    i, len_ref, qkv_ref, sink_ref, window_ref, summed_ref, stats_ref, heads_scr, stat_scr, extra_scr
):
    half = KVH * HD
    group = QH // KVH
    t = lax.axis_index("tp")
    slots = window_ref.shape[1]
    qkv = qkv_ref[i]
    fresh = qkv[:, QH * HD :]

    for h in range(QH):
        heads_scr[pl.ds(h, BR, stride=QH), :] = qkv[:, h * HD : (h + 1) * HD].astype(jnp.float32)
    for j in range(BR):
        extra_scr[j * SINK : (j + 1) * SINK, :] = sink_ref[i * BR + j].astype(jnp.float32)
    extra_scr[BR * SINK : BR * SINK + BR, :] = fresh.astype(jnp.float32)
    extra_scr[BR * SINK + BR :, :] = jnp.zeros_like(extra_scr[BR * SINK + BR :, :])
    extra = extra_scr[...].astype(jnp.bfloat16)
    head_row = lax.broadcasted_iota(jnp.int32, (BR * QH, HD), 0) % QH
    lane = lax.broadcasted_iota(jnp.int32, (BR * QH, HD), 1)
    first_half = head_row < group
    q = heads_scr[...]
    wide = jnp.concatenate([jnp.where(first_half, q, 0.0), jnp.where(first_half, 0.0, q)], axis=1)
    block = lambda array, j: array[j * QH : (j + 1) * QH]
    slot = t * slots + lax.broadcasted_iota(jnp.int32, (QH, slots), 1)
    lives, scores = [], []
    for j in range(BR):
        last = len_ref[i * BR + j] - 1
        back = jnp.bitwise_and(last - slot, WIN - 1)
        lives.append((last - back >= SINK) & (back != WIN - 1))
        raw = lax.dot_general(
            block(wide, j).astype(jnp.bfloat16), window_ref[i * BR + j, :, :half], NT,
            preferred_element_type=jnp.float32,
        )
        scores.append(jnp.where(lives[j], raw * HD ** (-0.5), NEG_BIG))
    s1 = jnp.concatenate(scores, axis=0)
    s2 = lax.dot_general(
        wide.astype(jnp.bfloat16), extra[:, :half], NT, preferred_element_type=jnp.float32
    ) * HD ** (-0.5)
    col = lax.broadcasted_iota(jnp.int32, s2.shape, 1)
    owner = lax.broadcasted_iota(jnp.int32, s2.shape, 0) // QH
    live2 = (jnp.where(col < BR * SINK, col // SINK, col - BR * SINK) == owner) & (t == 0)
    s2 = jnp.where(live2, s2, NEG_BIG)
    peak = jnp.maximum(jnp.max(s1, axis=1, keepdims=True), jnp.max(s2, axis=1, keepdims=True))
    w1 = jnp.exp(s1 - peak)
    w1 = jnp.concatenate([jnp.where(lives[j], block(w1, j), 0.0) for j in range(BR)], axis=0)
    w2 = jnp.where(live2, jnp.exp(s2 - peak), 0.0)
    total = jnp.sum(w1, axis=1, keepdims=True) + jnp.sum(w2, axis=1, keepdims=True)
    acc = jnp.concatenate(
        [
            jnp.dot(
                block(w1, j).astype(jnp.bfloat16), window_ref[i * BR + j, :, half:],
                preferred_element_type=jnp.float32,
            )
            for j in range(BR)
        ],
        axis=0,
    ) + jnp.dot(w2.astype(jnp.bfloat16), extra[:, half:], preferred_element_type=jnp.float32)
    heads_scr[...] = jnp.where(first_half, acc[:, :HD], acc[:, HD:])
    stat_scr[...] = jnp.where(lane == head_row, peak, 0.0) + jnp.where(
        lane == head_row + QH, total, 0.0
    )
    stats_ref[i] = functools.reduce(
        jnp.add, [stat_scr[pl.ds(h, BR, stride=QH), :] for h in range(QH)]
    )
    per_chunk = summed_ref.shape[3] // HD
    for h in range(QH):
        summed_ref[h // per_chunk, i, :, (h % per_chunk) * HD : (h % per_chunk + 1) * HD] = heads_scr[
            pl.ds(h, BR, stride=QH), :
        ].astype(jnp.bfloat16)


def scan_block(
    i, skip_ref, state_ref, coup_ref, projected_ref, taps_ref, conv_state_ref, step_ref, decay_ref,
    gated_ref, square_ref, step_x_ref,
):
    units = step_ref.shape[2]
    coup = coup_ref[i]
    out_rows = coup[:, NS:]
    in_f32 = coup[:, :NS].astype(jnp.float32)
    gate = projected_ref[0, i].astype(jnp.float32)
    x_pre = projected_ref[1, i]
    x = conv_rows([conv_state_ref[k, i] for k in range(3)], x_pre, taps_ref)
    step_x = step_ref[i] * x
    step_x_ref[i] = step_x
    decay = decay_ref[i]
    both = jnp.sum(in_f32 * out_rows.astype(jnp.float32), axis=1, keepdims=True)
    read_rows = []
    for j in range(BR):
        state = state_ref[i * BR + j]
        read_rows.append(
            lax.dot_general(out_rows, state, NT, preferred_element_type=jnp.float32)[j : j + 1, :]
        )
    readout = decay * jnp.concatenate(read_rows, axis=0) + step_x * both
    skip = jnp.concatenate(
        [by_head(skip_ref, g, (BR, 2 * MP)) for g in range(units // (2 * MP))], axis=1
    )
    gated = (readout + skip * x) * silu(gate)
    gated_ref[i] = gated
    square_ref[i] = jnp.broadcast_to(
        jnp.sum(gated * gated, axis=1, keepdims=True), square_ref.shape[1:]
    )


def update_block(i, state_ref, coup_ref, step_x_ref, decay_ref, new_state_ref):
    in_f32 = coup_ref[i][:, :NS].astype(jnp.float32)
    step_x_t = step_x_ref[i].T
    decay_t = decay_ref[i].T
    for j in range(BR):
        new_state_ref[i * BR + j] = (
            decay_t[:, j : j + 1] * state_ref[i * BR + j].astype(jnp.float32)
            + step_x_t[:, j : j + 1] * in_f32[j : j + 1, :]
        ).astype(jnp.bfloat16)


def ahead(array):
    return pltpu.with_memory_space_constraint(array, pltpu.VMEM)


def keep(array):
    return pltpu.with_memory_space_constraint(array, pltpu.HBM)


def other(index, k, size):
    total, bit = 0, 1
    while bit < size:
        a, b = lax.rem(lax.div(index, bit), 2), lax.rem(lax.div(k, bit), 2)
        total = total + bit * (a + b - 2 * a * b)
        bit *= 2
    return total


def joint_kernel(
    tp_size, req_size, len_ref, skip_ref, qkv_ref, sink_ref, window_ref, state_ref, coup_ref,
    projected_ref, taps_ref, conv_state_ref, step_ref, decay_ref, mixer_gain_ref, residual_ref,
    final_gain_ref, mamba_out_ref, attention_out_ref, head_ref, new_residual_ref, new_state_ref,
    logits_ref, heads_scr, stat_scr, extra_scr, summed_ref, stats_ref, gated_ref, square_ref,
    step_x_ref, square_buf, scan_out, scan_buf, mamba_buf, attention_buf, head_buf, sum_buf, stat_buf, part_out, part_buf, gather, final_buf,
    logit_out, square_s, square_r, scan_s, scan_r, sum_s, sum_r, stat_s, stat_r, part_s, part_r, gat_s, gat_r, log_s, log_r, load_sem,
):
    r = lax.axis_index("req")
    t = lax.axis_index("tp")
    rows = residual_ref.shape[0]
    blocks = rows // BR
    width = new_residual_ref.shape[1]
    peers = [other(t, q, tp_size) for q in range(tp_size)]
    reqs = [other(r, k, req_size) for k in range(req_size)]
    barrier = pltpu.get_barrier_semaphore()
    for q in range(1, tp_size):
        pl.semaphore_signal(barrier, inc=1, device_id=(r, peers[q]), device_id_type=MESH)
    for k in range(1, req_size):
        pl.semaphore_signal(barrier, inc=1, device_id=(reqs[k], t), device_id_type=MESH)
    load_mamba = pltpu.make_async_copy(mamba_out_ref, mamba_buf, load_sem.at[1])
    load_attention = pltpu.make_async_copy(attention_out_ref, attention_buf, load_sem.at[2])
    load_head = pltpu.make_async_copy(head_ref, head_buf, load_sem.at[3])
    for load in (load_mamba, load_attention, load_head):
        load.start()

    def attend(i, carry):
        attend_block(
            i, len_ref, qkv_ref, sink_ref, window_ref, summed_ref, stats_ref, heads_scr, stat_scr,
            extra_scr,
        )
        return carry

    lax.fori_loop(0, blocks, attend, 0)
    pl.semaphore_wait(barrier, tp_size + req_size - 2)

    def send(src, dst, ssem, rsem, where):
        copy = pltpu.make_async_remote_copy(
            src_ref=src, dst_ref=dst, send_sem=ssem, recv_sem=rsem,
            device_id=where, device_id_type=MESH,
        )
        copy.start()
        return copy

    first = []
    for q in reversed(range(1, tp_size)):
        where = (r, peers[q])
        first.append(send(stats_ref, stat_buf.at[q], stat_s.at[q], stat_r.at[q], where))
        first.append(send(summed_ref.at[peers[q]], sum_buf.at[q], sum_s.at[q], sum_r.at[q], where))

    def scan(i, carry):
        scan_block(
            i, skip_ref, state_ref, coup_ref, projected_ref, taps_ref, conv_state_ref, step_ref,
            decay_ref, gated_ref, square_ref, step_x_ref,
        )
        return carry

    lax.fori_loop(0, blocks, scan, 0)
    gated = gated_ref[...].reshape(rows, gated_ref.shape[2])
    mamba = (gated * mixer_gain_ref[...][None]).astype(jnp.bfloat16)
    columns = lambda p: pl.ds(pl.multiple_of(p * width, 128), width)
    load_mamba.wait()

    def unscaled(q):
        return jnp.dot(mamba, mamba_buf[:, columns(peers[q])], preferred_element_type=jnp.float32)

    between = []
    for q in reversed(range(1, tp_size)):
        where = (r, peers[q])
        between.append(send(square_ref, square_buf.at[q], square_s.at[q], square_r.at[q], where))
        scan_out[q] = unscaled(q).astype(jnp.bfloat16)
        between.append(send(scan_out.at[q], scan_buf.at[q], scan_s.at[q], scan_r.at[q], where))
    scanned = unscaled(0)
    load_attention.wait()
    for copy in first:
        copy.wait()
    flat = lambda array: array.astype(jnp.float32).reshape(rows, array.shape[2])
    stats = [flat(stats_ref[...])] + [flat(stat_buf[q]) for q in range(1, tp_size)]
    sums = [flat(summed_ref[t])] + [flat(sum_buf[q]) for q in range(1, tp_size)]
    lane = lax.broadcasted_iota(jnp.int32, (rows, 128), 1)
    local_heads = QH // tp_size
    pieces = []
    for hl in range(local_heads):
        h = t * local_heads + hl
        peaks = [jnp.sum(jnp.where(lane == h, s, 0.0), axis=1, keepdims=True) for s in stats]
        totals = [jnp.sum(jnp.where(lane == h + QH, s, 0.0), axis=1, keepdims=True) for s in stats]
        top = functools.reduce(jnp.maximum, peaks)
        scales = [jnp.exp(p - top) for p in peaks]
        below = functools.reduce(jnp.add, [a * b for a, b in zip(scales, totals)])
        above = functools.reduce(
            jnp.add, [a * b[:, hl * HD : (hl + 1) * HD] for a, b in zip(scales, sums)]
        )
        pieces.append((above / below).astype(jnp.bfloat16))
    attended = jnp.concatenate(pieces, axis=1)

    def partial(q):
        return jnp.dot(
            attended, attention_buf[:, columns(peers[q])], preferred_element_type=jnp.float32
        )

    second = {}
    for q in reversed(range(1, tp_size)):
        part_out[q] = partial(q).astype(jnp.bfloat16)
        second[q] = send(part_out.at[q], part_buf.at[q], part_s.at[q], part_r.at[q], (r, peers[q]))
    mixed = residual_ref[:, columns(t)].astype(jnp.float32) + partial(0)
    for copy in between:
        copy.wait()
    square = flat(square_ref[...])[:, :1]
    for q in range(1, tp_size):
        square = square + flat(square_buf[q])[:, :1]
        scanned = scanned + scan_buf[q].astype(jnp.float32)
    mixed = mixed + scanned * lax.rsqrt(square / (MH * MP) + EPSILON)
    for q in range(1, tp_size):
        second[q].wait()
        mixed = mixed + part_buf[q].astype(jnp.float32)
    fresh = mixed.astype(jnp.bfloat16)
    new_residual_ref[...] = fresh
    gather[0, 0] = fresh

    half = req_size // 2
    far_groups = list(range(half, req_size))
    near_groups = list(range(1, half))

    def move(k, src, dst, where):
        return pltpu.make_async_remote_copy(
            src_ref=gather.at[k if src else 0, src - 1 if src else 0], dst_ref=gather.at[k, dst],
            send_sem=gat_s.at[k, dst], recv_sem=gat_r.at[k, dst],
            device_id=where, device_id_type=MESH,
        )

    along = lambda k: move(k, 0, 0, (other(r, k, req_size), t))
    over = lambda k: move(k, 1, 2, (r, peers[2]))
    near = lambda k: move(k, 1, 1, (r, peers[1]))
    far = lambda k: move(k, 3, 3, (r, peers[1]))

    def spread(k):
        if k:
            along(k).wait_recv()
        over(k).start()
        near(k).start()

    def pair_up(k):
        over(k).wait_recv()
        far(k).start()

    along(half).start()
    for k in far_groups[1:] + near_groups:
        along(k).start()
    spread(half)
    spread(0)
    spread(half + 1)
    for k in near_groups:
        spread(k)
    pair_up(half)
    for k in far_groups[2:3]:
        spread(k)

    vocab = head_buf.shape[1]
    tile = min(1024, vocab)
    each = rows // tp_size
    source = r * tp_size + t

    def logits_to(k, q):
        return pltpu.make_async_remote_copy(
            src_ref=logit_out.at[k, peers[q]], dst_ref=logits_ref.at[source],
            send_sem=log_s.at[k, q], recv_sem=log_r.at[k, q],
            device_id=(other(r, k, req_size), peers[q]), device_id_type=MESH,
        )

    own = pltpu.make_async_copy(logit_out.at[0, t], logits_ref.at[source], load_sem.at[0])
    def group_at(n):
        late = lax.div(n, half)
        return (1 - late) * (n + half) + late * (req_size - 1 - n)

    load_head.wait()

    def project(n, carry):
        k = group_at(n)
        near(k).wait_recv()
        far(k).wait_recv()
        squares = jnp.zeros((rows, width), jnp.float32)
        for i in range(tp_size):
            value = gather[k, i].astype(jnp.float32)
            squares = squares + value * value
        mean = jnp.sum(squares, axis=1, keepdims=True) / (width * tp_size)
        scale = lax.rsqrt(mean + EPSILON)
        for i in range(tp_size):
            cols = columns(peers[i])
            final_buf[:, cols] = (
                gather[k, i].astype(jnp.float32) * scale * final_gain_ref[:, cols]
            ).astype(jnp.bfloat16)

        @pl.when(n + 1 < req_size)
        def _():
            pair_up(group_at(n + 1))

        def head_tile(c, carry):
            cols = pl.ds(pl.multiple_of(c * tile, 128), tile)
            part = jnp.dot(
                final_buf[...], head_buf[:, cols], preferred_element_type=jnp.float32
            )
            for q in range(tp_size):
                logit_out[k, q, :, cols] = part[q * each : (q + 1) * each, :].astype(jnp.bfloat16)
            return carry

        lax.fori_loop(0, vocab // tile, head_tile, 0)
        for q in reversed(range(1, tp_size)):
            logits_to(k, q).start()

        @pl.when(n != req_size - 1)
        def _():
            logits_to(k, 0).start()

        @pl.when(n == 0)
        def _():
            for later in far_groups[3:]:
                spread(later)

        @pl.when(n == req_size - 1)
        def _():
            own.start()

        return carry

    lax.fori_loop(0, req_size, project, 0)
    def update(i, carry):
        update_block(i, state_ref, coup_ref, step_x_ref, decay_ref, new_state_ref)
        return carry

    lax.fori_loop(0, blocks, update, 0)
    own.wait()

    def close(n, carry):
        k = group_at(n)
        for q in reversed(range(1, tp_size)):
            logits_to(k, q).wait()
        over(k).wait_send()
        near(k).wait_send()
        far(k).wait_send()

        @pl.when(n != req_size - 1)
        def _():
            logits_to(k, 0).wait()
            along(k).wait_send()

        return carry

    lax.fori_loop(0, req_size, close, 0)


def joint(
    lengths, skip, qkv, sink, window, state, coup, projected, taps, conv_state, step, decay,
    mixer_gain, mamba_out, attention_out, residual, final_gain, output_head,
):
    tp_size = lax.axis_size("tp")
    req_size = lax.axis_size("req")
    rows, model = residual.shape
    units = step.shape[1]
    blocks = rows // BR
    width = model // tp_size
    chunk = QH * HD // tp_size
    each = rows // tp_size
    vocab = output_head.shape[1]

    def split(a):
        at = a.ndim - 2
        return a.reshape(a.shape[:at] + (blocks, BR) + a.shape[at + 1 :])

    dma = lambda *shape: pltpu.SemaphoreType.DMA(shape)
    vmem = pl.BlockSpec(memory_space=pltpu.VMEM)
    smem = pl.BlockSpec(memory_space=pltpu.SMEM)
    hbm = pl.BlockSpec(memory_space=pltpu.HBM)
    return pl.pallas_call(
        functools.partial(joint_kernel, tp_size, req_size),
        in_specs=[smem] * 2 + [vmem] * 13 + [hbm] * 3,
        out_specs=[vmem, vmem, hbm],
        out_shape=[
            jax.ShapeDtypeStruct((rows, width), jnp.bfloat16),
            jax.ShapeDtypeStruct(state.shape, jnp.bfloat16),
            jax.ShapeDtypeStruct((req_size * tp_size, each, vocab), jnp.bfloat16),
        ],
        scratch_shapes=[
            pltpu.VMEM((BR * QH, HD), jnp.float32),
            pltpu.VMEM((BR * QH, HD), jnp.float32),
            pltpu.VMEM((BR * QH, 2 * KVH * HD), jnp.float32),
            pltpu.VMEM((tp_size, blocks, BR, chunk), jnp.bfloat16),
            pltpu.VMEM((blocks, BR, 128), jnp.float32),
            pltpu.VMEM((blocks, BR, units), jnp.float32),
            pltpu.VMEM((blocks, BR, 128), jnp.float32),
            pltpu.VMEM((blocks, BR, units), jnp.float32),
            pltpu.VMEM((tp_size, blocks, BR, 128), jnp.float32),
            pltpu.VMEM((tp_size, rows, width), jnp.bfloat16),
            pltpu.VMEM((tp_size, rows, width), jnp.bfloat16),
            pltpu.VMEM(mamba_out.shape, jnp.bfloat16),
            pltpu.VMEM(attention_out.shape, jnp.bfloat16),
            pltpu.VMEM(output_head.shape, jnp.bfloat16),
            pltpu.VMEM((tp_size, blocks, BR, chunk), jnp.bfloat16),
            pltpu.VMEM((tp_size, blocks, BR, 128), jnp.float32),
            pltpu.VMEM((tp_size, rows, width), jnp.bfloat16),
            pltpu.VMEM((tp_size, rows, width), jnp.bfloat16),
            pltpu.VMEM((req_size, tp_size, rows, width), jnp.bfloat16),
            pltpu.VMEM((rows, model), jnp.bfloat16),
            pltpu.VMEM((req_size, tp_size, each, vocab), jnp.bfloat16),
            dma(tp_size), dma(tp_size), dma(tp_size), dma(tp_size), dma(tp_size), dma(tp_size),
            dma(tp_size), dma(tp_size), dma(tp_size), dma(tp_size),
            dma(req_size, tp_size), dma(req_size, tp_size), dma(req_size, tp_size),
            dma(req_size, tp_size), dma(4),
        ],
        cost_estimate=pl.CostEstimate(
            flops=40_000_000_000, bytes_accessed=30_000_000, transcendentals=0
        ),
        compiler_params=pltpu.CompilerParams(
            collective_id=1, has_side_effects=True, vmem_limit_bytes=24 << 20
        ),
    )(
        lengths, skip, split(qkv), sink, ahead(window), ahead(state), split(coup), split(projected),
        taps, split(conv_state), split(step), split(decay), mixer_gain, residual, final_gain[None],
        keep(mamba_out), keep(attention_out), keep(output_head),
    )


def finish_kernel(
    residual_ref, blocks_ref, state_ref, conv_ref, projected_ref, coup_ref, pre_ref, qkv_ref,
    new_residual_ref, logits_ref, new_state_ref, new_conv_ref, new_coup_ref, key_value_ref, sem,
):
    part = state_ref.shape[0] // sem.shape[0]
    copies = [
        pltpu.make_async_copy(
            state_ref.at[pl.ds(n * part, part)], new_state_ref.at[pl.ds(n * part, part)], sem.at[n]
        )
        for n in range(sem.shape[0])
    ]
    step = pl.program_id(0)

    @pl.when(step == 0)
    def _():
        for copy in copies:
            copy.start()
        new_residual_ref[...] = residual_ref[...]
        new_conv_ref[0] = conv_ref[1]
        new_conv_ref[1] = conv_ref[2]
        new_conv_ref[2] = projected_ref[1]
        new_coup_ref[0] = coup_ref[1]
        new_coup_ref[1] = coup_ref[2]
        new_coup_ref[2] = pre_ref[...]
        key_value_ref[...] = qkv_ref[:, QH * HD :]

    width = blocks_ref.shape[2]
    for n in range(blocks_ref.shape[0]):
        logits_ref[:, n * width : (n + 1) * width] = blocks_ref[n].astype(jnp.float32)

    @pl.when(step == pl.num_programs(0) - 1)
    def _():
        for copy in copies:
            copy.wait()


def finish(residual, blocks, state, conv_state, projected, coup_state, pre, qkv):
    count, each, vocab = blocks.shape
    steps = 2
    part = count // steps
    shaped = lambda a: jax.ShapeDtypeStruct(a.shape, a.dtype)
    whole = lambda shape: pl.BlockSpec(shape, lambda i: (0,) * len(shape))
    key_value = (qkv.shape[0], qkv.shape[1] - QH * HD)
    return pl.pallas_call(
        finish_kernel,
        grid=(steps,),
        in_specs=[
            whole(residual.shape),
            pl.BlockSpec((part, each, vocab), lambda i: (i, 0, 0)),
            pl.BlockSpec(memory_space=pl.ANY),
            whole(conv_state.shape), whole(projected.shape), whole(coup_state.shape),
            whole(pre.shape), whole(qkv.shape),
        ],
        out_specs=[
            whole(residual.shape),
            pl.BlockSpec((each, part * vocab), lambda i: (0, i)),
            pl.BlockSpec(memory_space=pltpu.HBM),
            whole(conv_state.shape), whole(coup_state.shape), whole(key_value),
        ],
        out_shape=[
            shaped(residual),
            jax.ShapeDtypeStruct((each, count * vocab), jnp.float32),
            shaped(state), shaped(conv_state), shaped(coup_state),
            jax.ShapeDtypeStruct(key_value, qkv.dtype),
        ],
        scratch_shapes=[pltpu.SemaphoreType.DMA((4,))],
        compiler_params=pltpu.CompilerParams(vmem_limit_bytes=8 << 20),
    )(residual, blocks, state, conv_state, projected, coup_state, pre, qkv)


def body(
    residual,
    cache_lengths,
    input_gain,
    inner_weight,
    step_weight,
    step_bias,
    decay_log,
    skip_gain,
    conv_weight,
    conv_state,
    coupling_weight,
    coupling_conv,
    coupling_state,
    scan_state,
    mixer_gain,
    attention_weight,
    sink_cache,
    window_cache,
    mamba_out,
    attention_out,
    final_gain,
    output_head,
):
    row_count = residual.shape[0]
    local_units = inner_weight.shape[2]
    swap = lambda array: jnp.transpose(array, (1, 0, 2))
    coup_state = swap(coupling_state)
    normed, coupling_pre, qkv_rows, coupling_all, step_size, decay_rate = entry(
        step_bias, decay_log, residual, input_gain, attention_weight, coupling_weight,
        coupling_conv, coup_state, step_weight.T,
    )
    projected = jnp.einsum(
        "rd,dtc->trc", normed, inner_weight, preferred_element_type=jnp.float32
    ).astype(jnp.bfloat16)
    conv_rows_first = swap(conv_state)
    fresh_residual, fresh_state, blocks = joint(
        cache_lengths, skip_gain, qkv_rows, sink_cache, window_cache,
        scan_state.reshape(row_count, local_units, NS), coupling_all, projected, conv_weight,
        conv_rows_first, step_size, decay_rate, mixer_gain, mamba_out, attention_out, residual,
        final_gain, output_head,
    )
    new_residual, logits, new_state, new_conv, new_coup, new_key_value = finish(
        fresh_residual, blocks, fresh_state, conv_rows_first, projected, coup_state, coupling_pre,
        qkv_rows,
    )
    new_conv_state = swap(new_conv)
    new_coupling_state = swap(new_coup)
    new_scan_state = new_state.reshape(scan_state.shape)
    return (new_residual, logits, new_scan_state, new_conv_state, new_coupling_state, new_key_value)


def solution(mesh):
    return jax.shard_map(
        body,
        mesh=mesh,
        in_specs=(
            P("req", None),
            P("req"),
            P(),
            P(None, None, "tp"),
            P(None, "tp"),
            P("tp"),
            P("tp"),
            P("tp"),
            P(None, "tp"),
            P("req", None, "tp"),
            P(None, "tp"),
            P(None, "tp"),
            P("req", None, "tp"),
            P("req", "tp", None, None),
            P("tp"),
            P(None, "tp"),
            P("req", None, None),
            P("req", "tp", None),
            P("tp", None),
            P("tp", None),
            P(),
            P(None, ("req", "tp")),
        ),
        out_specs=(
            P("req", "tp"),
            P(("req", "tp"), None),
            P("req", "tp", None, None),
            P("req", None, "tp"),
            P("req", None, "tp"),
            P("req", None),
        ),
        check_vma=False,
    )
```
